32 devices in a mesh: depth: 8 (over y, x, core), tile: 4 (over z).
Axes of the slice: x: 2, y: 2, z: 4, core: 2. Of those that a mesh axis runs over, the one named last changes fastest.
Arguments:
- field: float32 [32, 384, 1024], P('depth', 'tile'), may hold values from -6 to 6
Outputs:
- image: float32 [4, 384, 1024], P(None, ('tile', 'depth'))
The draws below stay inside these ranges and needn't reach their ends.
All inputs are finite; a program needn't handle non-finite values.
Results may differ from the reference program's by a relative error of at most 0.0003.
Values sent between devices are 32-bit elements; how exact they have to be, the bound alone decides.
A program may use at most 64 MiB of HBM per device.

```python
import jax
import jax.numpy as jnp
from jax import lax

ROWS = 96
COLS = 1024
NZ = 32
HEIGHT = 384
N_TILE = 4


def level_of(key, extent, shards, least, high):
    gain, own = 1.0, jax.random.fold_in(key, 6)
    for position, shards_of in shards:
        steps = jnp.exp(jax.random.uniform(jax.random.fold_in(own, position), (shards_of,), jnp.float32, least / len(shards), high / len(shards)))
        gain = gain * jnp.repeat(steps, extent[position] // shards_of).reshape([-1 if axis == position else 1 for axis in range(len(extent))])
    return gain


def centred(rng, extent, width, limit, pieces=(), held_as=jnp.bfloat16):
    level = level_of(rng, extent, pieces, -0.22, 0.18) if pieces else 1.0
    result = jax.random.normal(rng, extent, jnp.float32) * width * level
    return jnp.minimum(jnp.maximum(result, -limit), limit).astype(held_as)


def setup_inputs(seed: int = 0) -> dict:
    key_of = jax.random.split(jax.random.key(seed), 2)
    field = centred(key_of[0], (NZ, HEIGHT, COLS), 1.0, 6.0, ((0, 8), (1, 4)), jnp.float32)
    return {"field": field}


centres = (-1.2, 0.3, 1.5)
spreads = (0.25, 0.35, 0.3)
heights = (2.0, 1.0, 3.0)
floor_density = 0.05
light_cols = 0.48
light_rows = 0.6
light_depth = 0.64

def emission(sample, slope_cols, slope_rows, slope_depth):
    density = floor_density + jnp.zeros_like(sample)
    for centre, spread, bump_height in zip(centres, spreads, heights):
        scaled = (sample - centre) / spread
        density = density + bump_height * jnp.exp(-scaled * scaled)
    facing = light_cols * slope_cols + light_rows * slope_rows + light_depth * slope_depth
    length = slope_cols * slope_cols + slope_rows * slope_rows + slope_depth * slope_depth + 1.0
    shading = 0.3 + 0.7 * jnp.abs(facing) * lax.rsqrt(length)
    colour = jnp.stack([shading * jax.nn.sigmoid(2.0 * sample), shading * jnp.exp(-sample * sample), shading * jax.nn.sigmoid(-2.0 * sample)])
    return (density, colour)

def integrate(density, colour, spacing):
    optics = spacing * density
    running = jnp.cumsum(optics, axis=0)
    before = jnp.concatenate([jnp.zeros_like(optics[:1]), running[:-1]], axis=0)
    weight = jnp.exp(-before) * -jnp.expm1(-optics)
    return (lax.optimization_barrier(jnp.sum(weight[None] * colour, axis=1)), jnp.exp(-running[-1]))

def reference(field):
    spacing = 3.0 / NZ
    height = field.shape[1]

    def one_block(block_index):
        first_row = block_index * ROWS
        has_below = (first_row > 0).astype(field.dtype)
        has_above = (first_row + ROWS < height).astype(field.dtype)
        row_below = lax.dynamic_slice_in_dim(field, jnp.maximum(first_row - 1, 0).astype(jnp.int32), 1, 1) * has_below
        middle = lax.dynamic_slice_in_dim(field, first_row.astype(jnp.int32), ROWS, 1)
        higher = lax.dynamic_slice_in_dim(field, jnp.minimum(first_row + ROWS, height - 1).astype(jnp.int32), 1, 1) * has_above
        window = jnp.concatenate([row_below, middle, higher], axis=1)
        further = jnp.concatenate([window[1:], jnp.zeros_like(window[:1])], axis=0)
        sample = 0.5 * (window + further)
        slope_depth = (further - window)[:, 1:-1]
        slope_rows = 0.5 * (sample[:, 2:] - sample[:, :-2])
        sample = sample[:, 1:-1]
        zero_col = jnp.zeros_like(sample[..., :1])
        slope_cols = 0.5 * (jnp.concatenate([sample[..., 1:], zero_col], axis=-1) - jnp.concatenate([zero_col, sample[..., :-1]], axis=-1))
        density, colour = emission(sample, slope_cols, slope_rows, slope_depth)
        colour_sum, through = integrate(density, colour, spacing)
        return jnp.concatenate([colour_sum, (1.0 - through)[None]], axis=0)
    blocks = lax.map(one_block, jnp.arange(N_TILE, dtype=jnp.int32))
    return jnp.transpose(blocks, (1, 0, 2, 3)).reshape(4, N_TILE * ROWS, field.shape[2])
```

```python
import functools
import math

import jax
import jax.numpy as jnp
from jax import lax
from jax.experimental import pallas as pl
from jax.experimental.pallas import tpu as pltpu
from jax.sharding import PartitionSpec as P

centres = (-1.2, 0.3, 1.5)
spreads = (0.25, 0.35, 0.3)
heights = (2.0, 1.0, 3.0)
floor_density = 0.05
light_cols = 0.48
light_rows = 0.6
light_depth = 0.64

LOG2E = math.log2(math.e)
SUB, LANE = 8, 128


def kernel(
    dims, field, out, behind, grid, corner_above, corner_below,
    parts, pair, own, pieces, result,
    raw_sem, plane_send_sem, plane_recv_sem, edge_send_sem, edge_recv_sem, pair_send_sem, pair_recv_sem,
    piece_send_sem, piece_recv_sem,
):
    planes, rows, cols, depth_count, tile_count = dims
    chips = depth_count // 2
    share = rows // depth_count
    spacing = 3.0 / (planes * depth_count)
    group = max(g for g in range(1, 5) if share % g == 0)
    me = lax.axis_index("depth")
    tile = lax.axis_index("tile")
    chip = me // 2
    core = me % 2
    partner = chip * 2 + (1 - core)
    stages = chips.bit_length() - 1
    assert chips == 1 << stages
    order = sorted(range(1, chips), key=lambda rel: (rel & -rel, -rel)) + [0]

    def relative(base, rel):
        for s in range(stages):
            if rel >> s & 1:
                base = base + (1 - 2 * (base // 2**s % 2)) * 2**s
        return base

    opposite = [relative(chip, 1 << s) * 2 + core for s in range(stages)]

    def remote(src, dst, send_sem, recv_sem, depth_to, tile_to):
        return pltpu.make_async_remote_copy(
            src_ref=src, dst_ref=dst, send_sem=send_sem, recv_sem=recv_sem,
            device_id=(depth_to, tile_to), device_id_type=pl.DeviceIdType.MESH,
        )

    loads = [
        [
            pltpu.make_async_copy(
                field.at[p, :, pl.ds(j * LANE, LANE)], grid.at[p, pl.ds(1, rows), j, :], raw_sem.at[p, j]
            )
            for j in range(cols // LANE)
        ]
        for p in range(planes)
    ]
    for plane in loads:
        for load in plane:
            load.start()

    has_front = me > 0
    has_behind = me < depth_count - 1
    has_low = tile > 0
    has_high = tile < tile_count - 1
    near = [
        (has_front, me - 1, tile),
        (has_behind, me + 1, tile),
        (has_low, me, tile - 1),
        (has_high, me, tile + 1),
        (has_front & has_low, me - 1, tile - 1),
        (has_front & has_high, me - 1, tile + 1),
        (has_behind & has_low, me + 1, tile - 1),
        (has_behind & has_high, me + 1, tile + 1),
    ]
    barrier = pltpu.get_barrier_semaphore()
    for cond, d, t in near:
        @pl.when(cond)
        def _(d=d, t=t):
            pl.semaphore_signal(barrier, inc=1, device_id=(d, t), device_id_type=pl.DeviceIdType.MESH)
    pl.semaphore_signal(barrier, inc=1, device_id=(partner, tile), device_id_type=pl.DeviceIdType.MESH)
    for other in opposite:
        pl.semaphore_signal(barrier, inc=1, device_id=(other, tile), device_id_type=pl.DeviceIdType.MESH)

    blank = jnp.zeros((SUB, LANE), jnp.float32)
    for cond, row in ((has_low, 0), (has_high, rows + 1)):
        @pl.when(jnp.logical_not(cond))
        def _(row=row):
            for p in range(planes):
                grid[p, row] = blank

    @pl.when(jnp.logical_not(has_behind))
    def _():
        for step in range(chips):
            behind[step] = jnp.zeros(behind.shape[1:], jnp.float32)

    greeted = 1 + stages
    for cond, _, _ in near:
        greeted = greeted + cond.astype(jnp.int32)
    for load in loads[0]:
        load.wait()
    pl.semaphore_wait(barrier, greeted)

    block = 2 * share
    sends = []

    def plane_row(row, count):
        return grid.at[0, pl.ds(row + 1, count)]

    strips = []
    to_chip = (me + depth_count - 1) // 2 % chips
    for step, rel in enumerate(order):
        q = relative(to_chip, rel)
        strip = []
        for k, (cond, row, count, place) in enumerate((
            (has_front, q * block, block, 1),
            (has_front & (q > 0), jnp.maximum(q * block - 1, 0), 1, 0),
            (has_front & (q < chips - 1), jnp.minimum((q + 1) * block, rows - 1), 1, block + 1),
        )):
            copy = remote(
                plane_row(row, count), behind.at[step, pl.ds(place, count)],
                plane_send_sem.at[step, k], plane_recv_sem.at[step, k], me - 1, tile,
            )
            sends.append((cond, copy))
            strip.append(copy)
        strips.append(strip)
    for cond, copy in sends:
        @pl.when(cond)
        def _(copy=copy):
            copy.start()

    to_low = remote(grid.at[:, 1], grid.at[:, rows + 1], edge_send_sem.at[0], edge_recv_sem.at[0], me, tile - 1)
    to_high = remote(grid.at[:, rows], grid.at[:, 0], edge_send_sem.at[1], edge_recv_sem.at[1], me, tile + 1)
    corner_low = remote(
        grid.at[0, 1], corner_above.at[...], edge_send_sem.at[2], edge_recv_sem.at[2], me - 1, tile - 1
    )
    corner_high = remote(
        grid.at[0, rows], corner_below.at[...], edge_send_sem.at[3], edge_recv_sem.at[3], me - 1, tile + 1
    )
    edges = [
        (has_low, to_low),
        (has_high, to_high),
        (has_front & has_low, corner_low),
        (has_front & has_high, corner_high),
    ]
    for plane in loads[1:]:
        for load in plane:
            load.wait()
    for cond, copy in edges:
        @pl.when(cond)
        def _(copy=copy):
            copy.start()

    lane = lax.broadcasted_iota(jnp.int32, (group, SUB, LANE), 2)
    sub = lax.broadcasted_iota(jnp.int32, (group, SUB, LANE), 1)
    left_edge = lane == 0
    right_edge = lane == LANE - 1
    left_end = left_edge & (sub == 0)
    right_end = right_edge & (sub == SUB - 1)
    scale = spacing * LOG2E

    def plane_step(p, row, state, there):
        red, blue, green, through = state
        here = grid[p, window(row)]
        total = here + there
        twice = total[1:-1]
        d_depth = there[1:-1] - here[1:-1]
        d_rows = total[2:] - total[:-2]
        from_left = pltpu.roll(twice, 1, 2)
        from_left = jnp.where(left_edge, pltpu.roll(from_left, 1, 1), from_left)
        from_left = jnp.where(left_end, 0.0, from_left)
        from_right = pltpu.roll(twice, LANE - 1, 2)
        from_right = jnp.where(right_edge, pltpu.roll(from_right, SUB - 1, 1), from_right)
        from_right = jnp.where(right_end, 0.0, from_right)
        d_cols = from_right - from_left
        facing = (0.25 * light_cols) * d_cols + (0.25 * light_rows) * d_rows + light_depth * d_depth
        length = (d_cols * d_cols + d_rows * d_rows) * 0.0625 + (d_depth * d_depth + 1.0)
        shading = 0.3 + 0.7 * jnp.abs(facing) * lax.rsqrt(length)
        optics = scale * floor_density
        for centre, width, bump in zip(centres, spreads, heights):
            root = math.sqrt(LOG2E) / width
            scaled = (0.5 * root) * twice - root * centre
            optics = optics + jnp.exp2(math.log2(bump * scale) - scaled * scaled)
        after = through * jnp.exp2(-optics)
        lit = (through - after) * shading
        middle = jnp.exp2((twice * (-0.25 * LOG2E)) * twice)
        balance = jnp.tanh(0.5 * twice)
        return (red + lit, blue + lit * balance, green + lit * middle, after)

    def put(rel, slot, offset, state):
        for c in range(4):
            parts[rel, slot, c, pl.ds(offset, group)] = state[c]

    zero = jnp.zeros((group, SUB, LANE), jnp.float32)
    per_share = share // group
    in_block = 2 * per_share

    def window(row):
        return pl.ds(row, group + 2)

    where = [relative(chip, rel) for rel in range(chips)]

    def early(rel):
        q = where[rel]
        turn = (q == 0).astype(jnp.int32)

        def body(i, carry):
            g = (i + turn) % in_block
            row = q * block + g * group
            state = (zero, zero, zero, zero + 1.0)
            for p in range(planes - 1):
                state = plane_step(p, row, state, grid[p + 1, window(row)])
            put(rel, (g // per_share + core + 1) % 2, g % per_share * group, state)
            return carry

        lax.fori_loop(0, in_block - 1, body, 0)
        pl.when((q == 0) & has_low)(to_high.wait_recv)
        pl.when((q == chips - 1) & has_high)(to_low.wait_recv)
        lax.fori_loop(in_block - 1, in_block, body, 0)

    def end(step, cond, have, copy, halo, place):
        @pl.when(cond & have)
        def _():
            copy.wait_recv()
            behind[step, place] = halo[...]

        @pl.when(cond & jnp.logical_not(have))
        def _():
            behind[step, place] = blank

    def arrive(step, rel):
        q = where[rel]
        whole, lower, upper = strips[step]
        pl.when(has_behind)(whole.wait_recv)
        pl.when(has_behind & (q > 0))(lower.wait_recv)
        pl.when(has_behind & (q < chips - 1))(upper.wait_recv)
        end(step, has_behind & (q == 0), has_low, corner_high, corner_below, 0)
        end(step, has_behind & (q == chips - 1), has_high, corner_low, corner_above, block + 1)

    def late(step, rel, slot):
        side = core if slot else 1 - core

        def body(i, carry):
            state = tuple(parts[rel, slot, c, pl.ds(i * group, group)] for c in range(4))
            place = side * share + i * group
            there = behind[step, window(place)]
            put(rel, slot, i * group, plane_step(planes - 1, where[rel] * block + place, state, there))
            return carry

        lax.fori_loop(0, per_share, body, 0)

    pair_copies = {}
    piece_copies = {}

    def compose(target, in_front, mine, theirs):
        mine = [mine[c] for c in range(4)]
        theirs = [theirs[c] for c in range(4)]
        through = jnp.where(in_front, mine[3], theirs[3])
        for c in range(3):
            target[c] = jnp.where(in_front, mine[c], theirs[c]) + through * jnp.where(in_front, theirs[c], mine[c])
        target[3] = mine[3] * theirs[3]

    def place_of(s, j):
        return chips - (chips >> s) + j

    def forward(s, rel):
        j = rel >> (s + 1)
        at = place_of(s, j)
        copy = remote(
            own.at[rel], pieces.at[at], piece_send_sem.at[at], piece_recv_sem.at[at], opposite[s], tile
        )
        copy.start()
        piece_copies[s, j] = copy

    def pair_send(rel):
        copy = remote(
            parts.at[rel, 0], pair.at[rel], pair_send_sem.at[rel], pair_recv_sem.at[rel], partner, tile
        )
        copy.start()
        pair_copies[rel] = copy

    def pair_merge(rel):
        pair_copies[rel].wait_recv()
        compose(own.at[rel], core == 0, parts.at[rel, 1], pair.at[rel])
        if rel % 2:
            forward(0, rel)

    ahead = 2
    for rel in order[:ahead]:
        early(rel)
    for step, rel in enumerate(order):
        arrive(step, rel)
        late(step, rel, 0)
        pair_send(rel)
        late(step, rel, 1)
        if step + ahead < chips:
            early(order[step + ahead])
        elif step > 0 and step - 1 + ahead >= chips:
            pair_merge(order[step - 1])
        if step + ahead < chips:
            pair_merge(rel)
    pair_merge(order[-1])

    for s in range(stages):
        for j in reversed(range(chips >> (s + 1))):
            rel = j << (s + 1)
            piece_copies[s, j].wait_recv()
            compose(own.at[rel], chip // 2**s % 2 == 0, own.at[rel], pieces.at[place_of(s, j)])
            if j % 2:
                forward(s + 1, rel)
    colour = [own[0, c] for c in range(3)]
    through = own[0, 3]
    image = (0.5 * (colour[0] + colour[1]), colour[2], 0.5 * (colour[0] - colour[1]), through)
    for c in range(4):
        result[:, c * SUB : (c + 1) * SUB, :] = image[c]
    for j in range(cols // LANE):
        out[:, :, j * LANE : (j + 1) * LANE] = result[:, pl.ds(j, 4, stride=SUB), :]

    for copy in [*pair_copies.values(), *piece_copies.values()]:
        copy.wait_send()
    for cond, copy in edges + sends:
        @pl.when(cond)
        def _(copy=copy):
            copy.wait_send()


def local(field):
    planes, rows, cols = field.shape
    depth_count = lax.axis_size("depth")
    chips = depth_count // 2
    share = rows // depth_count
    f32 = jnp.float32
    dims = (planes, rows, cols, depth_count, lax.axis_size("tile"))
    dma = pltpu.SemaphoreType.DMA
    image = pl.pallas_call(
        functools.partial(kernel, dims),
        out_shape=jax.ShapeDtypeStruct((share, 4, cols), f32),
        in_specs=[pl.BlockSpec(memory_space=pltpu.HBM)],
        out_specs=pl.BlockSpec(memory_space=pltpu.VMEM),
        scratch_shapes=[
            pltpu.VMEM((chips, 2 * share + 2, SUB, LANE), f32),
            pltpu.VMEM((planes, rows + 2, SUB, LANE), f32),
            pltpu.VMEM((SUB, LANE), f32),
            pltpu.VMEM((SUB, LANE), f32),
            pltpu.VMEM((chips, 2, 4, share, SUB, LANE), f32),
            pltpu.VMEM((chips, 4, share, SUB, LANE), f32),
            pltpu.VMEM((chips, 4, share, SUB, LANE), f32),
            pltpu.VMEM((chips, 4, share, SUB, LANE), f32),
            pltpu.VMEM((share, 4 * SUB, LANE), f32),
            dma((planes, cols // LANE)),
            dma((chips, 3)),
            dma((chips, 3)),
            dma((4,)),
            dma((4,)),
            dma((chips,)),
            dma((chips,)),
            dma((chips,)),
            dma((chips,)),
        ],
        compiler_params=pltpu.CompilerParams(
            collective_id=0, has_side_effects=True, vmem_limit_bytes=55_000_000
        ),
    )(field)
    image = jnp.transpose(image, (1, 0, 2))
    channel = lax.broadcasted_iota(jnp.int32, image.shape, 0)
    return jnp.where(channel == 3, 1.0 - image, image)


def solution(mesh):
    return jax.shard_map(
        local,
        mesh=mesh,
        in_specs=(P("depth", "tile", None),),
        out_specs=P(None, ("tile", "depth"), None),
        check_vma=False,
    )
```

```python
import functools
import math

import jax
import jax.numpy as jnp
from jax import lax
from jax.experimental import pallas as pl
from jax.experimental.pallas import tpu as pltpu
from jax.sharding import PartitionSpec as P

centres = (-1.2, 0.3, 1.5)
spreads = (0.25, 0.35, 0.3)
heights = (2.0, 1.0, 3.0)
floor_density = 0.05
light_cols = 0.48
light_rows = 0.6
light_depth = 0.64

LOG2E = math.log2(math.e)
SUB, LANE = 8, 128


def divide(chips):
    def at(c, q):
        if c == chips - 1 or q == chips - 2 - c:
            return 1
        if q == chips - 1 - c:
            return 0
        return q % 2 if c % 2 else int(2 * c >= chips)

    behind = [[at(c, q) for q in range(chips)] for c in range(chips)]
    front = [[0] * chips] + [[1 - b for b in behind[c]] for c in range(chips - 1)]
    return front, behind


def kernel(
    dims, field, out, grid, own, pieces, result,
    load_sem, pair_send_sem, pair_recv_sem, plane_send_sem, plane_recv_sem, edge_send_sem, edge_recv_sem,
    corner_send_sem, corner_recv_sem, piece_send_sem, piece_recv_sem,
):
    planes, rows, cols, depth_count, tile_count = dims
    chips = depth_count // 2
    share = rows // depth_count
    block = 2 * share
    spacing = 3.0 / (planes * depth_count)
    group = max(g for g in range(1, 5) if share % g == 0)
    groups = share // group
    me = lax.axis_index("depth")
    tile = lax.axis_index("tile")
    chip = me // 2
    core = me % 2
    stages = chips.bit_length() - 1
    assert chips == 1 << stages
    order = sorted(range(1, chips), key=lambda rel: (rel & -rel, -rel)) + [0]
    last = 2 * planes
    mine = pl.ds(1 + core * planes, planes)

    def relative(base, rel):
        for s in range(stages):
            if rel >> s & 1:
                base = base + (1 - 2 * (base // 2**s % 2)) * 2**s
        return base

    def look(values, at):
        total = 0
        for c, value in enumerate(values):
            if value:
                total = total + (at == c).astype(jnp.int32)
        return total > 0 if any(values) else at < 0

    table = divide(chips)

    def assigned(kind, at, rel):
        return look([table[kind][c][c ^ rel] for c in range(chips)], at)

    def assigned_row(kind, at, q):
        return look([table[kind][c][q] for c in range(chips)], at)

    def remote(src, dst, send_sem, recv_sem, chip_to, core_to, tile_to):
        return pltpu.make_async_remote_copy(
            src_ref=src, dst_ref=dst, send_sem=send_sem, recv_sem=recv_sem,
            device_id=(chip_to * 2 + core_to, tile_to), device_id_type=pl.DeviceIdType.MESH,
        )

    def load(p):
        return [
            pltpu.make_async_copy(
                field.at[p, :, pl.ds(j * LANE, LANE)], grid.at[1 + core * planes + p, pl.ds(1, rows), j, :],
                load_sem.at[p, j],
            )
            for j in range(cols // LANE)
        ]

    turned = [core * (planes - 1) + p * (1 - 2 * core) for p in range(planes)]
    loads = [load(p) for p in turned]
    for copies in loads:
        for copy in copies:
            copy.start()

    has_front = chip > 0
    has_behind = chip < chips - 1
    has_low = tile > 0
    has_high = tile < tile_count - 1
    beside = tile - 1 + 2 * core
    has_beside = jnp.where(core == 0, has_low, has_high)
    meets = chip - 1 + 2 * core
    has_meets = jnp.where(core == 0, has_front, has_behind)
    meets = jnp.where(has_meets, meets, chip)
    opposite = [relative(chip, 1 << s) for s in range(stages)]

    barrier = pltpu.get_barrier_semaphore()

    def greet(cond, c, k, t):
        @pl.when(cond)
        def _():
            pl.semaphore_signal(barrier, inc=1, device_id=(c * 2 + k, t), device_id_type=pl.DeviceIdType.MESH)

    always = chip >= 0
    for c in opposite:
        greet(always, c, core, tile)
    greet(has_beside, chip, 0, beside)
    greet(has_beside, chip, 1, beside)
    greet(has_behind, chip + 1, 0, tile)
    greet(has_front, chip - 1, 1, tile)
    greet(has_behind & has_beside, chip + 1, 0, beside)
    greet(has_front & has_beside, chip - 1, 1, beside)
    greet(always, chip, 1 - core, tile)

    def count(cond):
        return cond.astype(jnp.int32)

    greeted = (
        1 + stages + 2 * count(has_meets) + count(has_high) + count(has_low)
        + count(has_meets & has_high) + count(has_meets & has_low)
    )

    blank = jnp.zeros((SUB, LANE), jnp.float32)

    @pl.when(jnp.logical_not(has_beside))
    def _():
        row = core * (rows + 1)
        for p in range(last + 2):
            grid[p, row] = blank

    @pl.when(jnp.logical_not(has_behind))
    def _():
        grid[last + 1] = jnp.zeros(grid.shape[1:], jnp.float32)

    for copy in loads[0]:
        copy.wait()
    pl.semaphore_wait(barrier, greeted)

    def is_end(q, k):
        return jnp.where(k == 0, q == 0, q == chips - 1)

    def windows(cond, q, k, make):
        start = q * block + k * share
        whole = make(pl.ds(start, share + 2))
        inner = make(pl.ds(jnp.maximum(start, 1), share + 1))
        end = is_end(q, k)
        return [(cond & jnp.logical_not(end), whole), (cond & end, inner)]

    def begin(copies):
        for cond, copy in copies:
            pl.when(cond)(copy.start)
        return copies

    from_plane = 1 + core * (last - 1)
    to_plane = (1 - core) * (last + 1)
    sent = []
    for step, rel in enumerate(order):
        q = relative(meets, rel)
        due = has_meets & jnp.where(core == 0, assigned(1, meets, rel), assigned(0, meets, rel))
        for k in range(2):
            sent += begin(windows(due, q, k, lambda at: remote(
                grid.at[from_plane, at], grid.at[to_plane, at],
                plane_send_sem.at[k, step], plane_recv_sem.at[core, step], meets, k, tile,
            )))

    for copies in loads[1:]:
        for copy in copies:
            copy.wait()

    def swap(step, rel, k):
        return windows(always, relative(chip, rel), k, lambda at: remote(
            grid.at[mine, at], grid.at[mine, at], pair_send_sem.at[step], pair_recv_sem.at[step], chip, 1 - core, tile
        ))

    outer = ((rows, 0, 0, tile + 1, has_high), (1, rows + 1, 1, tile - 1, has_low))
    sent += begin(swap(0, order[0], 1 - core))
    for row, to_row, k, t, have in outer:
        sent += begin([(have, remote(
            grid.at[mine, row], grid.at[mine, to_row], edge_send_sem.at[k], edge_recv_sem.at[core], chip, k, t
        ))])
    for row, to_row, k, t, have in outer:
        q = k * (chips - 1)
        due = has_meets & have & jnp.where(core == 0, assigned_row(1, meets, q), assigned_row(0, meets, q))
        sent += begin([(due, remote(
            grid.at[from_plane, row], grid.at[to_plane, to_row], corner_send_sem.at[k], corner_recv_sem.at[core],
            meets, k, t,
        ))])
    for step, rel in enumerate(order[1:], 1):
        sent += begin(swap(step, rel, 1 - core))

    lane = lax.broadcasted_iota(jnp.int32, (group, SUB, LANE), 2)
    sub = lax.broadcasted_iota(jnp.int32, (group, SUB, LANE), 1)
    left_edge = lane == 0
    right_edge = lane == LANE - 1
    left_end = left_edge & (sub == 0)
    right_end = right_edge & (sub == SUB - 1)
    scale = spacing * LOG2E

    def window(row):
        return pl.ds(row, group + 2)

    def plane_step(p, row, state):
        red, blue, green, through = state
        here = grid[p, window(row)]
        there = grid[p + 1, window(row)]
        total = here + there
        twice = total[1:-1]
        d_depth = there[1:-1] - here[1:-1]
        d_rows = total[2:] - total[:-2]
        from_left = pltpu.roll(twice, 1, 2)
        from_left = jnp.where(left_edge, pltpu.roll(from_left, 1, 1), from_left)
        from_left = jnp.where(left_end, 0.0, from_left)
        from_right = pltpu.roll(twice, LANE - 1, 2)
        from_right = jnp.where(right_edge, pltpu.roll(from_right, SUB - 1, 1), from_right)
        from_right = jnp.where(right_end, 0.0, from_right)
        d_cols = from_right - from_left
        facing = (0.25 * light_cols) * d_cols + (0.25 * light_rows) * d_rows + light_depth * d_depth
        length = (d_cols * d_cols + d_rows * d_rows) * 0.0625 + (d_depth * d_depth + 1.0)
        shading = 0.3 + 0.7 * jnp.abs(facing) * lax.rsqrt(length)
        optics = scale * floor_density
        for centre, width, bump in zip(centres, spreads, heights):
            root = math.sqrt(LOG2E) / width
            scaled = (0.5 * root) * twice - root * centre
            optics = optics + jnp.exp2(math.log2(bump * scale) - scaled * scaled)
        after = through * jnp.exp2(-optics)
        lit = (through - after) * shading
        middle = jnp.exp2((twice * (-0.25 * LOG2E)) * twice)
        balance = jnp.tanh(0.5 * twice)
        return (red + lit, blue + lit * balance, green + lit * middle, after)

    zero = jnp.zeros((group, SUB, LANE), jnp.float32)
    clear = (zero, zero, zero, zero + 1.0)
    far = core * (rows + 1)

    def from_partner(step, rel):
        there = pl.ds(1 + (1 - core) * planes, planes)
        return windows(always, relative(chip, rel), core, lambda at: remote(
            grid.at[there, at], grid.at[there, at], pair_send_sem.at[step], pair_recv_sem.at[step], chip, 1 - core, tile
        ))

    def from_neighbour(kind, cond, step, rel):
        return windows(cond, relative(chip, rel), core, lambda at: remote(
            grid.at[1, at], grid.at[1, at], plane_send_sem.at[0, step], plane_recv_sem.at[kind, step], chip, 1 - core, tile
        ))

    def edge(k):
        there = pl.ds(1 + k * planes, planes)
        return remote(
            grid.at[there, far], grid.at[there, far], edge_send_sem.at[0], edge_recv_sem.at[k], chip, 1 - core, tile
        )

    def corner(kind):
        return remote(
            grid.at[1, far], grid.at[1, far], corner_send_sem.at[0], corner_recv_sem.at[kind], chip, 1 - core, tile
        )

    def arrived(copies):
        for cond, copy in copies:
            pl.when(cond)(copy.wait_recv)

    def get(rel, at):
        return tuple(own[rel, c, at] for c in range(4))

    def put(rel, at, state):
        for c in range(4):
            own[rel, c, at] = state[c]

    def inside(step, rel):
        q = relative(chip, rel)
        end = is_end(q, core)
        turn = count(end & (core == 0))
        arrived(from_partner(step, rel))

        def body(i, carry):
            for k in range(2):
                pl.when(end & has_beside & (i == groups - 1))(edge(k).wait_recv)
            offset = (i + turn) % groups * group
            row = q * block + core * share + offset
            state = clear
            for p in range(1, last):
                state = plane_step(p, row, state)
            put(rel, pl.ds(offset, group), state)
            return carry

        lax.fori_loop(0, groups, body, 0)

    def interface(step, rel):
        q = relative(chip, rel)
        start = q * block + core * share
        end = is_end(q, core)
        ahead = assigned(0, chip, rel)
        after = assigned(1, chip, rel)

        @pl.when(ahead)
        def _():
            arrived(from_neighbour(1, ahead, step, rel))
            pl.when(end & has_beside)(corner(1).wait_recv)

            def body(i, carry):
                at = pl.ds(i * group, group)
                red, blue, green, through = get(rel, at)
                first = plane_step(0, start + i * group, clear)
                put(rel, at, (
                    first[0] + first[3] * red, first[1] + first[3] * blue, first[2] + first[3] * green,
                    first[3] * through,
                ))
                return carry

            lax.fori_loop(0, groups, body, 0)

        @pl.when(after)
        def _():
            arrived(from_neighbour(0, has_behind, step, rel))
            pl.when(has_behind & end & has_beside)(corner(0).wait_recv)

            def body(i, carry):
                at = pl.ds(i * group, group)
                put(rel, at, plane_step(last, start + i * group, get(rel, at)))
                return carry

            lax.fori_loop(0, groups, body, 0)

    piece_copies = {}

    def forward(s, rel):
        j = rel >> (s + 1)
        at = chips - (chips >> s) + j
        copy = remote(
            own.at[rel], pieces.at[at], piece_send_sem.at[at], piece_recv_sem.at[at], opposite[s], core, tile
        )
        copy.start()
        sent.append((always, copy))
        piece_copies[s, j] = (copy, at)

    for step, rel in enumerate(order):
        inside(step, rel)
        interface(step, rel)
        if rel % 2:
            forward(0, rel)

    for s in range(stages):
        nearer = chip // 2**s % 2 == 0
        for j in reversed(range(chips >> (s + 1))):
            rel = j << (s + 1)
            copy, at = piece_copies[s, j]
            copy.wait_recv()
            here = [own[rel, c] for c in range(4)]
            there = [pieces[at, c] for c in range(4)]
            through = jnp.where(nearer, here[3], there[3])
            for c in range(3):
                own[rel, c] = jnp.where(nearer, here[c], there[c]) + through * jnp.where(nearer, there[c], here[c])
            own[rel, 3] = here[3] * there[3]
            if j % 2:
                forward(s + 1, rel)
    colour = [own[0, c] for c in range(3)]
    through = own[0, 3]
    image = (0.5 * (colour[0] + colour[1]), colour[2], 0.5 * (colour[0] - colour[1]), through)
    for c in range(4):
        result[:, c * SUB : (c + 1) * SUB, :] = image[c]
    for j in range(cols // LANE):
        out[:, :, j * LANE : (j + 1) * LANE] = result[:, pl.ds(j, 4, stride=SUB), :]

    for cond, copy in sent:
        pl.when(cond)(copy.wait_send)


def local(field):
    planes, rows, cols = field.shape
    depth_count = lax.axis_size("depth")
    chips = depth_count // 2
    share = rows // depth_count
    f32 = jnp.float32
    dims = (planes, rows, cols, depth_count, lax.axis_size("tile"))
    dma = pltpu.SemaphoreType.DMA
    image = pl.pallas_call(
        functools.partial(kernel, dims),
        out_shape=jax.ShapeDtypeStruct((share, 4, cols), f32),
        in_specs=[pl.BlockSpec(memory_space=pltpu.HBM)],
        out_specs=pl.BlockSpec(memory_space=pltpu.VMEM),
        scratch_shapes=[
            pltpu.VMEM((2 * planes + 2, rows + 2, SUB, LANE), f32),
            pltpu.VMEM((chips, 4, share, SUB, LANE), f32),
            pltpu.VMEM((chips - 1, 4, share, SUB, LANE), f32),
            pltpu.VMEM((share, 4 * SUB, LANE), f32),
            dma((planes, cols // LANE)),
            dma((chips,)),
            dma((chips,)),
            dma((2, chips)),
            dma((2, chips)),
            dma((2,)),
            dma((2,)),
            dma((2,)),
            dma((2,)),
            dma((chips - 1,)),
            dma((chips - 1,)),
        ],
        compiler_params=pltpu.CompilerParams(
            collective_id=0, has_side_effects=True, vmem_limit_bytes=55_000_000
        ),
    )(field)
    image = jnp.transpose(image, (1, 0, 2))
    channel = lax.broadcasted_iota(jnp.int32, image.shape, 0)
    return jnp.where(channel == 3, 1.0 - image, image)


def solution(mesh):
    return jax.shard_map(
        local,
        mesh=mesh,
        in_specs=(P("depth", "tile", None),),
        out_specs=P(None, ("tile", "depth"), None),
        check_vma=False,
    )
```

```python
import functools
import math

import jax
import jax.numpy as jnp
from jax import lax
from jax.experimental import pallas as pl
from jax.experimental.pallas import tpu as pltpu
from jax.sharding import PartitionSpec as P

centres = (-1.2, 0.3, 1.5)
spreads = (0.25, 0.35, 0.3)
heights = (2.0, 1.0, 3.0)
floor_density = 0.05
light_cols = 0.48
light_rows = 0.6
light_depth = 0.64

LOG2E = math.log2(math.e)
SUB, LANE = 8, 128


def kernel(
    dims, field, out, grid, own, pieces, result,
    load_sem, pair_send_sem, pair_recv_sem, outer_send_sem, outer_recv_sem, edge_send_sem, edge_recv_sem,
    plane_send_sem, plane_recv_sem, piece_send_sem, piece_recv_sem,
):
    planes, rows, cols, depth_count, tile_count, groups = dims
    chips = depth_count // 2
    share = rows // depth_count
    block = 2 * share
    spacing = 3.0 / (planes * depth_count)
    group = share // groups
    me = lax.axis_index("depth")
    tile = lax.axis_index("tile")
    chip = me // 2
    core = me % 2
    stages = chips.bit_length() - 1
    assert chips == 1 << stages
    order = sorted(range(1, chips), key=lambda rel: (rel & -rel, -rel)) + [0]
    last = 2 * planes
    mine = pl.ds(1 + core * planes, planes)

    def relative(base, rel):
        for s in range(stages):
            if rel >> s & 1:
                base = base + (1 - 2 * (base // 2**s % 2)) * 2**s
        return base

    def remote(src, dst, send_sem, recv_sem, chip_to=chip, core_to=core, tile_to=tile):
        return pltpu.make_async_remote_copy(
            src_ref=src, dst_ref=dst, send_sem=send_sem, recv_sem=recv_sem,
            device_id=(chip_to * 2 + core_to, tile_to), device_id_type=pl.DeviceIdType.MESH,
        )

    def load(p):
        return [
            pltpu.make_async_copy(
                field.at[p, :, pl.ds(j * LANE, LANE)], grid.at[1 + core * planes + p, pl.ds(1, rows), j, :],
                load_sem.at[p, j],
            )
            for j in range(cols // LANE)
        ]

    turned = [core * (planes - 1) + p * (1 - 2 * core) for p in range(planes)]
    loads = [load(p) for p in turned]
    for copies in loads:
        for copy in copies:
            copy.start()

    has_front = chip > 0
    has_behind = chip < chips - 1
    has_low = tile > 0
    has_high = tile < tile_count - 1
    has_beside = jnp.where(core == 0, has_low, has_high)
    gives = jnp.where(core == 0, has_high, has_low)
    beside = tile - 1 + 2 * core
    opposite = [relative(chip, 1 << s) for s in range(stages)]
    odd = chip % 2
    has_far = jnp.where(odd == 0, has_front, has_behind)
    far_chip = jnp.where(has_far, chip - 1 + 2 * odd, chip)

    barrier = pltpu.get_barrier_semaphore()

    def greet(cond, c, k, t):
        @pl.when(cond)
        def _():
            pl.semaphore_signal(barrier, inc=1, device_id=(c * 2 + k, t), device_id_type=pl.DeviceIdType.MESH)

    always = chip >= 0
    greet(has_beside, chip, core, beside)
    greet(has_far, far_chip, core, tile)
    for c in opposite:
        greet(always, c, core, tile)
    greet(always, chip, 1 - core, tile)

    def count(cond):
        return cond.astype(jnp.int32)

    blank = jnp.zeros((SUB, LANE), jnp.float32)
    far = core * (rows + 1)

    @pl.when(jnp.logical_not(has_beside))
    def _():
        for p in range(1, last + 1):
            grid[p, far] = blank

    @pl.when(jnp.logical_not(has_behind))
    def _():
        grid[last + 1] = jnp.zeros(grid.shape[1:], jnp.float32)

    for copy in loads[0]:
        copy.wait()
    pl.semaphore_wait(barrier, 1 + stages + count(has_far) + count(gives))

    sent = []

    def begin(cond, copy):
        pl.when(cond)(copy.start)
        sent.append((cond, copy))

    def is_end(q, k):
        return jnp.where(k == 0, q == 0, q == chips - 1)

    evens = range(0, chips, 2)
    next_chip = [jnp.where(has_front, chip - 1, chip), jnp.where(has_behind, chip + 1, chip)]
    has_next = [has_front, has_behind]

    def window_of(q, k):
        return pl.ds(q * block + k * share, share + 2)

    def neighbour(kind, rel, at):
        return remote(
            grid.at[1 + kind * (last - 1), at], grid.at[(1 - kind) * (last + 1), at],
            plane_send_sem.at[kind, rel // 2], plane_recv_sem.at[kind, rel // 2], next_chip[kind],
        )

    planes_out = []
    for rel in reversed(evens):
        for kind in range(2):
            q = relative(next_chip[kind], rel)
            planes_out.append((kind, has_next[kind], is_end(q, core), neighbour(kind, rel, window_of(q, core))))

    for kind, cond, end, copy in planes_out:
        begin(cond & jnp.logical_not(end) & (core == kind), copy)

    for copies in loads[1:]:
        for copy in copies:
            copy.wait()

    def swap(step, rel, k, which):
        q = relative(chip, rel)
        start = q * block + k * share
        end = is_end(q, k)
        return [
            (cond, remote(
                grid.at[which, at], grid.at[which, at], pair_send_sem.at[step], pair_recv_sem.at[step], core_to=1 - core
            ))
            for cond, at in (
                (jnp.logical_not(end), pl.ds(start, share + 2)),
                (end, pl.ds(jnp.maximum(start, 1), share + 1)),
            )
        ]

    theirs = pl.ds(1 + (1 - core) * planes, planes)

    def outer(which, k):
        row = rows - k * (rows - 1)
        return remote(
            grid.at[which, row], grid.at[which, row], outer_send_sem.at[0], outer_recv_sem.at[0], core_to=1 - core
        )

    every = pl.ds(1, last)
    edge = remote(
        grid.at[every, rows - core * (rows - 1)], grid.at[every, far], edge_send_sem.at[0], edge_recv_sem.at[0],
        tile_to=tile + 1 - 2 * core,
    )
    begin(always, outer(mine, 1 - core))
    for step, rel in enumerate(order):
        for cond, copy in swap(step, rel, 1 - core, mine):
            begin(cond, copy)
    outer(theirs, core).wait_recv()
    begin(gives, edge)
    for step, rel in enumerate(order):
        for cond, copy in swap(step, rel, core, theirs):
            pl.when(cond)(copy.wait_recv)
    for kind, cond, end, copy in planes_out:
        begin(cond & jnp.logical_not(end) & (core != kind), copy)

    lane = lax.broadcasted_iota(jnp.int32, (group, SUB, LANE), 2)
    sub = lax.broadcasted_iota(jnp.int32, (group, SUB, LANE), 1)
    left_edge = lane == 0
    right_edge = lane == LANE - 1
    left_end = left_edge & (sub == 0)
    right_end = right_edge & (sub == SUB - 1)
    scale = spacing * LOG2E

    def window(row):
        return pl.ds(row, group + 2)

    def plane_step(p, row, state):
        red, blue, green, through = state
        here = grid[p, window(row)]
        there = grid[p + 1, window(row)]
        total = here + there
        twice = total[1:-1]
        d_depth = there[1:-1] - here[1:-1]
        d_rows = total[2:] - total[:-2]
        from_left = pltpu.roll(twice, 1, 2)
        from_left = jnp.where(left_edge, pltpu.roll(from_left, 1, 1), from_left)
        from_left = jnp.where(left_end, 0.0, from_left)
        from_right = pltpu.roll(twice, LANE - 1, 2)
        from_right = jnp.where(right_edge, pltpu.roll(from_right, SUB - 1, 1), from_right)
        from_right = jnp.where(right_end, 0.0, from_right)
        d_cols = from_right - from_left
        facing = (0.25 * light_cols) * d_cols + (0.25 * light_rows) * d_rows + light_depth * d_depth
        length = (d_cols * d_cols + d_rows * d_rows) * 0.0625 + (d_depth * d_depth + 1.0)
        shading = 0.3 + 0.7 * jnp.abs(facing) * lax.rsqrt(length)
        optics = scale * floor_density
        for centre, width, bump in zip(centres, spreads, heights):
            root = math.sqrt(LOG2E) / width
            scaled = (0.5 * root) * twice - root * centre
            optics = optics + jnp.exp2(math.log2(bump * scale) - scaled * scaled)
        after = through * jnp.exp2(-optics)
        lit = (through - after) * shading
        middle = jnp.exp2((twice * (-0.25 * LOG2E)) * twice)
        balance = jnp.tanh(0.5 * twice)
        return (red + lit, blue + lit * balance, green + lit * middle, after)

    zero = jnp.zeros((group, SUB, LANE), jnp.float32)
    clear = (zero, zero, zero, zero + 1.0)
    def get(rel, at):
        return tuple(own[rel, c, at] for c in range(4))

    def put(rel, at, state):
        for c in range(4):
            own[rel, c, at] = state[c]

    def inside(rel, first):
        q = relative(chip, rel)
        end = is_end(q, core)
        turn = count(end & (core == 0))

        def body(i, carry):
            if first:
                pl.when(end & has_beside & (i == groups - 1))(edge.wait_recv)
            offset = (i + turn) % groups * group
            row = q * block + core * share + offset
            state = clear
            for p in range(1, last):
                state = plane_step(p, row, state)
            put(rel, pl.ds(offset, group), state)
            return carry

        lax.fori_loop(0, groups, body, 0)
        if first:
            pl.when(jnp.logical_not(end) & has_beside)(edge.wait_recv)

    def in_front(rel):
        start = relative(chip, rel) * block + core * share

        @pl.when(has_front)
        def _():
            neighbour(1, rel, window_of(0, 0)).wait_recv()

            def body(i, carry):
                at = pl.ds(i * group, group)
                red, blue, green, through = get(rel, at)
                first = plane_step(0, start + i * group, clear)
                put(rel, at, (
                    first[0] + first[3] * red, first[1] + first[3] * blue, first[2] + first[3] * green,
                    first[3] * through,
                ))
                return carry

            lax.fori_loop(0, groups, body, 0)

    def behind(rel, cond):
        start = relative(chip, rel) * block + core * share

        @pl.when(cond)
        def _():
            def body(i, carry):
                at = pl.ds(i * group, group)
                put(rel, at, plane_step(last, start + i * group, get(rel, at)))
                return carry

            lax.fori_loop(0, groups, body, 0)

    piece_copies = {}

    def forward(s, rel, i):
        j = rel >> (s + 1)
        slot = chips - (chips >> s) + j
        at = pl.ds(i * group, group)
        copy = remote(
            own.at[rel, :, at], pieces.at[slot, :, at], piece_send_sem.at[slot, i], piece_recv_sem.at[slot, i],
            opposite[s],
        )
        begin(always, copy)
        piece_copies[s, j, i] = (copy, slot)

    for step, rel in enumerate(order):
        inside(rel, step == 0)
        if step == 0:
            for kind, cond, end, copy in planes_out:
                begin(cond & end, copy)
        if rel % 2:
            behind(rel, jnp.logical_not(has_behind))
            for i in range(groups):
                forward(0, rel, i)
    for rel in reversed(evens):
        in_front(rel)
        pl.when(has_behind)(neighbour(0, rel, window_of(0, 0)).wait_recv)
        behind(rel, always)

    for s in range(stages):
        nearer = chip // 2**s % 2 == 0
        for j in reversed(range(chips >> (s + 1))):
            rel = j << (s + 1)
            for i in range(groups):
                at = pl.ds(i * group, group)
                copy, slot = piece_copies[s, j, i]
                copy.wait_recv()
                here = get(rel, at)
                there = [pieces[slot, c, at] for c in range(4)]
                through = jnp.where(nearer, here[3], there[3])
                state = [
                    jnp.where(nearer, here[c], there[c]) + through * jnp.where(nearer, there[c], here[c])
                    for c in range(3)
                ]
                state.append(here[3] * there[3])
                if s < stages - 1:
                    put(rel, at, state)
                    if j % 2:
                        forward(s + 1, rel, i)
                else:
                    image = (0.5 * (state[0] + state[1]), state[2], 0.5 * (state[0] - state[1]), state[3])
                    for c in range(4):
                        result[at, c * SUB : (c + 1) * SUB, :] = image[c]
    for j in range(cols // LANE):
        out[:, :, j * LANE : (j + 1) * LANE] = result[:, pl.ds(j, 4, stride=SUB), :]

    for cond, copy in sent:
        pl.when(cond)(copy.wait_send)


def local(field):
    planes, rows, cols = field.shape
    depth_count = lax.axis_size("depth")
    chips = depth_count // 2
    share = rows // depth_count
    f32 = jnp.float32
    groups = min(share // g for g in range(1, 5) if share % g == 0)
    dims = (planes, rows, cols, depth_count, lax.axis_size("tile"), groups)
    dma = pltpu.SemaphoreType.DMA
    image = pl.pallas_call(
        functools.partial(kernel, dims),
        out_shape=jax.ShapeDtypeStruct((share, 4, cols), f32),
        in_specs=[pl.BlockSpec(memory_space=pltpu.HBM)],
        out_specs=pl.BlockSpec(memory_space=pltpu.VMEM),
        scratch_shapes=[
            pltpu.VMEM((2 * planes + 2, rows + 2, SUB, LANE), f32),
            pltpu.VMEM((chips, 4, share, SUB, LANE), f32),
            pltpu.VMEM((chips - 1, 4, share, SUB, LANE), f32),
            pltpu.VMEM((share, 4 * SUB, LANE), f32),
            dma((planes, cols // LANE)),
            dma((chips,)),
            dma((chips,)),
            dma((1,)),
            dma((1,)),
            dma((1,)),
            dma((1,)),
            dma((2, chips // 2)),
            dma((2, chips // 2)),
            dma((chips - 1, groups)),
            dma((chips - 1, groups)),
        ],
        compiler_params=pltpu.CompilerParams(
            collective_id=0, has_side_effects=True, vmem_limit_bytes=55_000_000
        ),
    )(field)
    image = jnp.transpose(image, (1, 0, 2))
    channel = lax.broadcasted_iota(jnp.int32, image.shape, 0)
    return jnp.where(channel == 3, 1.0 - image, image)


def solution(mesh):
    return jax.shard_map(
        local,
        mesh=mesh,
        in_specs=(P("depth", "tile", None),),
        out_specs=P(None, ("tile", "depth"), None),
        check_vma=False,
    )
```

```python
import functools
import math

import jax
import jax.numpy as jnp
from jax import lax
from jax.experimental import pallas as pl
from jax.experimental.pallas import tpu as pltpu
from jax.sharding import PartitionSpec as P

centres = (-1.2, 0.3, 1.5)
spreads = (0.25, 0.35, 0.3)
heights = (2.0, 1.0, 3.0)
floor_density = 0.05
light_cols = 0.48
light_rows = 0.6
light_depth = 0.64

LOG2E = math.log2(math.e)
SUB, LANE = 8, 128
RELAY = ((3,), (3,))


def kernel(
    dims, field, out, grid, own, pieces, passing, result,
    load_sem, pair_send_sem, pair_recv_sem, edge_send_sem, edge_recv_sem,
    plane_send_sem, plane_recv_sem, passing_send_sem, passing_recv_sem, piece_send_sem, piece_recv_sem,
):
    planes, rows, cols, depth_count, tile_count, groups = dims
    chips = depth_count // 2
    share = rows // depth_count
    block = 2 * share
    spacing = 3.0 / (planes * depth_count)
    group = share // groups
    me = lax.axis_index("depth")
    tile = lax.axis_index("tile")
    chip = me // 2
    core = me % 2
    stages = chips.bit_length() - 1
    assert chips == 1 << stages
    order = sorted(range(1, chips), key=lambda rel: (rel & -rel, -rel)) + [0]
    last = 2 * planes
    mine = pl.ds(1 + core * planes, planes)

    def relative(base, rel):
        for s in range(stages):
            if rel >> s & 1:
                base = base + (1 - 2 * (base // 2**s % 2)) * 2**s
        return base

    def remote(src, dst, send_sem, recv_sem, chip_to=chip, core_to=core, tile_to=tile):
        return pltpu.make_async_remote_copy(
            src_ref=src, dst_ref=dst, send_sem=send_sem, recv_sem=recv_sem,
            device_id=(chip_to * 2 + core_to, tile_to), device_id_type=pl.DeviceIdType.MESH,
        )

    has_front = chip > 0
    has_behind = chip < chips - 1
    has_low = tile > 0
    has_high = tile < tile_count - 1
    opposite = [relative(chip, 1 << s) for s in range(stages)]
    odd = chip % 2
    has_far = jnp.where(odd == 0, has_front, has_behind)
    far_chip = jnp.where(has_far, chip - 1 + 2 * odd, chip)

    barrier = pltpu.get_barrier_semaphore()

    def greet(cond, c, k, t):
        @pl.when(cond)
        def _():
            pl.semaphore_signal(barrier, inc=1, device_id=(c * 2 + k, t), device_id_type=pl.DeviceIdType.MESH)

    always = chip >= 0
    has_beside = jnp.where(core == 0, has_low, has_high)
    beside = tile - 1 + 2 * core
    far = core * (rows + 1)
    greet(has_beside, chip, 0, beside)
    greet(has_beside, chip, 1, beside)
    greet(has_far, far_chip, core, tile)
    for c in opposite:
        greet(always, c, core, tile)
    greet(always, chip, 1 - core, tile)

    def count(cond):
        return cond.astype(jnp.int32)

    blank = jnp.zeros((SUB, LANE), jnp.float32)

    def load(p, count, k):
        return [
            pltpu.make_async_copy(
                field.at[pl.ds(p, count), :, pl.ds(j * LANE, LANE)],
                grid.at[pl.ds(1 + core * planes + p, count), pl.ds(1, rows), j, :],
                load_sem.at[k, j],
            )
            for j in range(cols // LANE)
        ]

    loads = [load(core * (planes - 1), 1, 0), load(1 - core, planes - 1, 1)]
    for copies in loads:
        for copy in copies:
            copy.start()

    @pl.when(jnp.logical_not(has_beside))
    def _():
        for p in range(1, last + 1):
            grid[p, far] = blank

    @pl.when(jnp.logical_not(has_behind))
    def _():
        grid[last + 1] = jnp.zeros(grid.shape[1:], jnp.float32)

    for copy in loads[0]:
        copy.wait()
    pl.semaphore_wait(barrier, 1 + stages + count(has_far) + count(has_low) + count(has_high))

    sent = []

    def begin(cond, copy):
        pl.when(cond)(copy.start)
        sent.append((cond, copy))

    def is_end(q, k):
        return jnp.where(k == 0, q == 0, q == chips - 1)

    evens = range(0, chips, 2)
    next_chip = [jnp.where(has_front, chip - 1, chip), jnp.where(has_behind, chip + 1, chip)]
    has_next = [has_front, has_behind]

    where = [relative(chip, rel) for rel in range(chips)]
    odds = [rel for rel in order if rel % 2]

    def window_of(q, k):
        return pl.ds(q * block + k * share, share + 2)

    def neighbour(kind, q):
        at = window_of(q, core)
        return remote(
            grid.at[1 + kind * (last - 1), at], grid.at[(1 - kind) * (last + 1), at],
            plane_send_sem.at[kind, q // 2], plane_recv_sem.at[kind, q // 2], next_chip[kind],
        )

    quarter = chip % 4
    turns = (RELAY if stages > 1 else ((), ()))

    def planes_out(rel, kind, cond):
        q = where[rel]
        cond = cond & has_next[kind]
        if rel % 4 in turns[kind]:
            around = quarter == 2 - kind
            slot = rel // 2
            begin(cond & around, remote(
                grid.at[1 + kind * (last - 1), window_of(q, core)], passing.at[slot],
                plane_send_sem.at[kind, q // 2], passing_recv_sem.at[slot], opposite[1],
            ))
            cond = cond & jnp.logical_not(around)
        begin(cond, neighbour(kind, q))

    def pass_on(rel):
        for kind in range(2):
            if rel % 4 in turns[kind]:
                slot = rel // 2
                at = window_of(relative(opposite[1], rel), core)
                q = relative(opposite[1], rel)
                copy = remote(
                    passing.at[slot], grid.at[(1 - kind) * (last + 1), at],
                    passing_send_sem.at[slot], plane_recv_sem.at[kind, q // 2], opposite[0],
                )
                arriving = remote(
                    passing.at[slot], passing.at[slot], passing_send_sem.at[slot], passing_recv_sem.at[slot], opposite[1]
                )
                cond = quarter == 3 * kind
                pl.when(cond)(arriving.wait_recv)
                begin(cond, copy)

    for rel in odds:
        for kind in range(2):
            planes_out(rel, kind, jnp.logical_not(is_end(where[rel], core)) & (core == kind))

    for copies in loads[1:]:
        for copy in copies:
            copy.wait()

    theirs = pl.ds(1 + (1 - core) * planes, planes)

    def swap(step, rel, k, which):
        start = where[rel] * block + k * share
        end = is_end(where[rel], k)
        return [
            (cond, remote(
                grid.at[which, at], grid.at[which, at], pair_send_sem.at[step], pair_recv_sem.at[step], core_to=1 - core
            ))
            for cond, at in (
                (jnp.logical_not(end), pl.ds(start, share + 2)),
                (end, pl.ds(jnp.maximum(start, 1), share + 1)),
            )
        ]

    def swapped(step, rel):
        for cond, copy in swap(step, rel, core, theirs):
            pl.when(cond)(copy.wait_recv)

    for step, rel in enumerate(order):
        for cond, copy in swap(step, rel, 1 - core, mine):
            begin(cond, copy)
        if step == 0:
            for k, (have, row, t) in enumerate(((has_high, rows, tile + 1), (has_low, 1, tile - 1))):
                begin(have, remote(
                    grid.at[mine, row], grid.at[mine, k * (rows + 1)], edge_send_sem.at[k], edge_recv_sem.at[core],
                    core_to=k, tile_to=t,
                ))

    def edges(cond):
        for k in range(2):
            which = pl.ds(1 + k * planes, planes)
            copy = remote(
                grid.at[which, far], grid.at[which, far], edge_send_sem.at[0], edge_recv_sem.at[k], core_to=1 - core
            )
            pl.when(cond & has_beside)(copy.wait_recv)

    lane = lax.broadcasted_iota(jnp.int32, (group, SUB, LANE), 2)
    sub = lax.broadcasted_iota(jnp.int32, (group, SUB, LANE), 1)
    left_edge = lane == 0
    right_edge = lane == LANE - 1
    left_end = left_edge & (sub == 0)
    right_end = right_edge & (sub == SUB - 1)
    scale = spacing * LOG2E

    def window(row):
        return pl.ds(row, group + 2)

    def plane_step(p, row, state):
        red, blue, green, through = state
        here = grid[p, window(row)]
        there = grid[p + 1, window(row)]
        total = here + there
        twice = total[1:-1]
        d_depth = there[1:-1] - here[1:-1]
        d_rows = total[2:] - total[:-2]
        from_left = pltpu.roll(twice, 1, 2)
        from_left = jnp.where(left_edge, pltpu.roll(from_left, 1, 1), from_left)
        from_left = jnp.where(left_end, 0.0, from_left)
        from_right = pltpu.roll(twice, LANE - 1, 2)
        from_right = jnp.where(right_edge, pltpu.roll(from_right, SUB - 1, 1), from_right)
        from_right = jnp.where(right_end, 0.0, from_right)
        d_cols = from_right - from_left
        facing = (0.25 * light_cols) * d_cols + (0.25 * light_rows) * d_rows + light_depth * d_depth
        length = (d_cols * d_cols + d_rows * d_rows) * 0.0625 + (d_depth * d_depth + 1.0)
        shading = 0.3 + 0.7 * jnp.abs(facing) * lax.rsqrt(length)
        optics = scale * floor_density
        for centre, width, bump in zip(centres, spreads, heights):
            root = math.sqrt(LOG2E) / width
            scaled = (0.5 * root) * twice - root * centre
            optics = optics + jnp.exp2(math.log2(bump * scale) - scaled * scaled)
        after = through * jnp.exp2(-optics)
        lit = (through - after) * shading
        middle = jnp.exp2((twice * (-0.25 * LOG2E)) * twice)
        balance = jnp.tanh(0.5 * twice)
        return (red + lit, blue + lit * balance, green + lit * middle, after)

    zero = jnp.zeros((group, SUB, LANE), jnp.float32)
    clear = (zero, zero, zero, zero + 1.0)
    def get(rel, at):
        return tuple(own[rel, c, at] for c in range(4))

    def put(rel, at, state):
        for c in range(4):
            own[rel, c, at] = state[c]

    def place(rel, i):
        turn = count(is_end(where[rel], core) & (core == 0))
        offset = (i + turn) % groups * group
        return pl.ds(offset, group), where[rel] * block + core * share + offset

    def near_state(row):
        state = clear
        for p in range(planes - 1):
            state = plane_step(1 + core * planes + p, row, state)
        return state

    def near_part(rel, low, high):
        def body(i, carry):
            at, row = place(rel, i)
            put(rel, at, near_state(row))
            return carry

        lax.fori_loop(low, high, body, 0)

    def compose(nearer, here, there):
        through = jnp.where(nearer, here[3], there[3])
        state = [
            jnp.where(nearer, here[c], there[c]) + through * jnp.where(nearer, there[c], here[c]) for c in range(3)
        ]
        return (*state, here[3] * there[3])

    def far_part(rel, low, high, both):
        def body(i, carry):
            at, row = place(rel, i)
            here = near_state(row) if both else get(rel, at)
            state = clear
            for p in range(planes):
                state = plane_step(planes - (planes - 1) * core + p, row, state)
            put(rel, at, compose(core == 0, here, state))
            return carry

        lax.fori_loop(low, high, body, 0)

    def in_front(rel):
        start = where[rel] * block + core * share

        @pl.when(has_front)
        def _():
            neighbour(1, where[rel]).wait_recv()

            def body(i, carry):
                at = pl.ds(i * group, group)
                red, blue, green, through = get(rel, at)
                first = plane_step(0, start + i * group, clear)
                put(rel, at, (
                    first[0] + first[3] * red, first[1] + first[3] * blue, first[2] + first[3] * green,
                    first[3] * through,
                ))
                return carry

            lax.fori_loop(0, groups, body, 0)

    def behind(rel, cond):
        start = where[rel] * block + core * share

        @pl.when(cond)
        def _():
            def body(i, carry):
                at = pl.ds(i * group, group)
                put(rel, at, plane_step(last, start + i * group, get(rel, at)))
                return carry

            lax.fori_loop(0, groups, body, 0)

    piece_copies = {}

    def forward(s, rel, i):
        j = rel >> (s + 1)
        slot = chips - (chips >> s) + j
        at = pl.ds(i * group, group)
        copy = remote(
            own.at[rel, :, at], pieces.at[slot, :, at], piece_send_sem.at[slot, i], piece_recv_sem.at[slot, i],
            opposite[s],
        )
        begin(always, copy)
        piece_copies[s, j, i] = (copy, slot)

    for rel in order[:2]:
        near_part(rel, 0, groups - 1)
    for step, rel in enumerate(odds):
        swapped(step, rel)
        for kind in range(2):
            planes_out(rel, kind, jnp.logical_not(is_end(where[rel], core)) & (core != kind))
    for step, rel in enumerate(order):
        if rel % 2 == 0:
            swapped(step, rel)
        if step < 2:
            far_part(rel, 0, groups - 1, False)
        if step == 0:
            edges(is_end(where[rel], core))
        far_part(rel, groups - 1 if step < 2 else 0, groups, True)
        if step == 0:
            edges(jnp.logical_not(is_end(where[rel], core)))
            for odd_rel in odds:
                for kind in range(2):
                    planes_out(odd_rel, kind, is_end(where[odd_rel], core))
        if rel % 2:
            behind(rel, jnp.logical_not(has_behind))
            if step >= 1:
                pass_on(order[step - 1])
            for i in range(groups):
                forward(0, rel, i)
    pass_on(odds[-1])

    def interfaces(rel):
        in_front(rel)
        pl.when(has_behind)(neighbour(0, where[rel]).wait_recv)
        behind(rel, always)

    for s in range(stages):
        nearer = chip // 2**s % 2 == 0
        for j in reversed(range(chips >> (s + 1))):
            rel = j << (s + 1)
            if s == 0:
                interfaces(rel)
            for i in range(groups):
                at = pl.ds(i * group, group)
                copy, slot = piece_copies[s, j, i]
                copy.wait_recv()
                state = compose(nearer, get(rel, at), [pieces[slot, c, at] for c in range(4)])
                if s < stages - 1:
                    put(rel, at, state)
                    if j % 2:
                        forward(s + 1, rel, i)
                else:
                    image = (0.5 * (state[0] + state[1]), state[2], 0.5 * (state[0] - state[1]), state[3])
                    for c in range(4):
                        result[at, c * SUB : (c + 1) * SUB, :] = image[c]
                    for b in range(cols // LANE):
                        out[at, :, b * LANE : (b + 1) * LANE] = result[at, pl.ds(b, 4, stride=SUB), :]

    for cond, copy in sent:
        pl.when(cond)(copy.wait_send)


def local(field):
    planes, rows, cols = field.shape
    depth_count = lax.axis_size("depth")
    chips = depth_count // 2
    share = rows // depth_count
    f32 = jnp.float32
    groups = min(share // g for g in range(1, 5) if share % g == 0)
    dims = (planes, rows, cols, depth_count, lax.axis_size("tile"), groups)
    dma = pltpu.SemaphoreType.DMA
    image = pl.pallas_call(
        functools.partial(kernel, dims),
        out_shape=jax.ShapeDtypeStruct((share, 4, cols), f32),
        in_specs=[pl.BlockSpec(memory_space=pltpu.HBM)],
        out_specs=pl.BlockSpec(memory_space=pltpu.VMEM),
        scratch_shapes=[
            pltpu.VMEM((2 * planes + 2, rows + 2, SUB, LANE), f32),
            pltpu.VMEM((chips, 4, share, SUB, LANE), f32),
            pltpu.VMEM((chips - 1, 4, share, SUB, LANE), f32),
            pltpu.VMEM((chips // 2, share + 2, SUB, LANE), f32),
            pltpu.VMEM((share, 4 * SUB, LANE), f32),
            dma((2, cols // LANE)),
            dma((chips,)),
            dma((chips,)),
            dma((2,)),
            dma((2,)),
            dma((2, chips // 2)),
            dma((2, chips // 2)),
            dma((chips // 2,)),
            dma((chips // 2,)),
            dma((chips - 1, groups)),
            dma((chips - 1, groups)),
        ],
        compiler_params=pltpu.CompilerParams(
            collective_id=0, has_side_effects=True, vmem_limit_bytes=55_000_000
        ),
    )(field)
    image = jnp.transpose(image, (1, 0, 2))
    channel = lax.broadcasted_iota(jnp.int32, image.shape, 0)
    return jnp.where(channel == 3, 1.0 - image, image)


def solution(mesh):
    return jax.shard_map(
        local,
        mesh=mesh,
        in_specs=(P("depth", "tile", None),),
        out_specs=P(None, ("tile", "depth"), None),
        check_vma=False,
    )
```

```python
import functools
import math

import jax
import jax.numpy as jnp
from jax import lax
from jax.experimental import pallas as pl
from jax.experimental.pallas import tpu as pltpu
from jax.sharding import PartitionSpec as P

centres = (-1.2, 0.3, 1.5)
spreads = (0.25, 0.35, 0.3)
heights = (2.0, 1.0, 3.0)
floor_density = 0.05
light_cols = 0.48
light_rows = 0.6
light_depth = 0.64

LOG2E = math.log2(math.e)
SUB, LANE = 8, 128
RELAY = (3,)
AHEAD = 4


def kernel(
    dims, field, out, grid, own, pieces, passing, result,
    load_sem, pair_send_sem, pair_recv_sem, edge_send_sem, edge_recv_sem,
    plane_send_sem, plane_recv_sem, passing_send_sem, passing_recv_sem, halo_send_sem, halo_recv_sem,
    piece_send_sem, piece_recv_sem,
):
    planes, rows, cols, depth_count, tile_count, groups = dims
    chips = depth_count // 2
    share = rows // depth_count
    block = 2 * share
    spacing = 3.0 / (planes * depth_count)
    group = share // groups
    me = lax.axis_index("depth")
    tile = lax.axis_index("tile")
    chip = me // 2
    core = me % 2
    stages = chips.bit_length() - 1
    assert chips == 1 << stages
    order = sorted(range(1, chips), key=lambda rel: (rel & -rel, -rel)) + [0]
    last = 2 * planes
    mine = pl.ds(1 + core * planes, planes)

    def relative(base, rel):
        for s in range(stages):
            if rel >> s & 1:
                base = base + (1 - 2 * (base // 2**s % 2)) * 2**s
        return base

    def remote(src, dst, send_sem, recv_sem, chip_to=chip, core_to=core, tile_to=tile):
        return pltpu.make_async_remote_copy(
            src_ref=src, dst_ref=dst, send_sem=send_sem, recv_sem=recv_sem,
            device_id=(chip_to * 2 + core_to, tile_to), device_id_type=pl.DeviceIdType.MESH,
        )

    has_front = chip > 0
    has_behind = chip < chips - 1
    has_low = tile > 0
    has_high = tile < tile_count - 1
    opposite = [relative(chip, 1 << s) for s in range(stages)]
    odd = chip % 2
    has_far = jnp.where(odd == 0, has_front, has_behind)
    far_chip = jnp.where(has_far, chip - 1 + 2 * odd, chip)

    barrier = pltpu.get_barrier_semaphore()

    def greet(cond, c, k, t):
        @pl.when(cond)
        def _():
            pl.semaphore_signal(barrier, inc=1, device_id=(c * 2 + k, t), device_id_type=pl.DeviceIdType.MESH)

    always = chip >= 0
    has_beside = jnp.where(core == 0, has_low, has_high)
    beside = tile - 1 + 2 * core
    far = core * (rows + 1)
    greet(has_beside, chip, 0, beside)
    greet(has_beside, chip, 1, beside)
    greet(has_far & (core == odd), far_chip, 1 - core, tile)
    greet(has_far, far_chip, core, tile)
    greet(always, opposite[0], 1 - core, tile)
    for c in opposite:
        greet(always, c, core, tile)
    greet(always, chip, 1 - core, tile)

    def count(cond):
        return cond.astype(jnp.int32)

    blank = jnp.zeros((SUB, LANE), jnp.float32)

    def load(p, count, k):
        return [
            pltpu.make_async_copy(
                field.at[pl.ds(p, count), :, pl.ds(j * LANE, LANE)],
                grid.at[pl.ds(1 + core * planes + p, count), pl.ds(1, rows), j, :],
                load_sem.at[k, j],
            )
            for j in range(cols // LANE)
        ]

    loads = [load(core * (planes - 1), 1, 0), load(1 - core, planes - 1, 1)]
    for copies in loads:
        for copy in copies:
            copy.start()

    @pl.when(jnp.logical_not(has_beside))
    def _():
        for p in range(last + 2):
            grid[p, far] = blank

    @pl.when(jnp.logical_not(has_behind))
    def _():
        grid[last + 1] = jnp.zeros(grid.shape[1:], jnp.float32)

    for copy in loads[0]:
        copy.wait()
    pl.semaphore_wait(barrier, 2 + stages + count(has_far) + count(has_far & (core == odd)) + count(has_low) + count(has_high))

    sent = []

    def begin(cond, copy):
        if cond is always:
            copy.start()
        else:
            pl.when(cond)(copy.start)
        sent.append((cond, copy))

    def drain():
        for cond, copy in sent:
            if cond is always:
                copy.wait_send()
            else:
                pl.when(cond)(copy.wait_send)
        sent.clear()

    def is_end(q, k):
        return jnp.where(k == 0, q == 0, q == chips - 1)

    evens = range(0, chips, 2)
    next_chip = [jnp.where(has_front, chip - 1, chip), jnp.where(has_behind, chip + 1, chip)]
    has_next = [has_front, has_behind]

    where = [relative(chip, rel) for rel in range(chips)]
    odds = [rel for rel in order if rel % 2]

    def windows(q, k):
        start = q * block + k * share
        end = is_end(q, k)
        skip = count(start == 0)
        return [
            (jnp.logical_not(end), pl.ds(start, share + 2), pl.ds(0, share + 2)),
            (end, pl.ds(start + skip, share + 1), pl.ds(skip, share + 1)),
        ]

    from_plane = 1 + core * (last - 1)
    to_plane = (1 - core) * (last + 1)
    meets = jnp.where(core == 0, next_chip[0], next_chip[1])
    has_meets = jnp.where(core == 0, has_front, has_behind)
    quarter = chip % 4
    turns = RELAY if stages > 1 else ()

    def planes_out(rel, k):
        q = where[rel]
        around = (quarter == 2 - core) & has_meets if rel % 4 in turns else chip < 0
        slot = rel // 2
        for cond, at, local_at in windows(q, k):
            if rel % 4 in turns:
                begin(cond & around, remote(
                    grid.at[from_plane, at], passing.at[k, slot, local_at],
                    plane_send_sem.at[k, slot], passing_recv_sem.at[k, slot], opposite[1],
                ))
            begin(cond & has_meets & jnp.logical_not(around), remote(
                grid.at[from_plane, at], grid.at[to_plane, at],
                plane_send_sem.at[k, slot], plane_recv_sem.at[core, q // 2], meets, k,
            ))

    def pass_on(rel):
        if rel % 4 not in turns:
            return
        slot = rel // 2
        q = relative(opposite[1], rel)
        for k in range(2):
            for cond, at, local_at in windows(q, k):
                cond = cond & (quarter == 3 * core)
                arriving = remote(
                    passing.at[k, slot, local_at], passing.at[k, slot, local_at],
                    passing_send_sem.at[k, slot], passing_recv_sem.at[k, slot], opposite[1],
                )
                pl.when(cond)(arriving.wait_recv)
                begin(cond, remote(
                    passing.at[k, slot, local_at], grid.at[to_plane, at],
                    passing_send_sem.at[k, slot], plane_recv_sem.at[core, q // 2], opposite[0], k,
                ))

    def halo(kind):
        return remote(
            grid.at[1 + kind * (last - 1), far], grid.at[(1 - kind) * (last + 1), far],
            halo_send_sem.at[kind], halo_recv_sem.at[kind], next_chip[kind],
        )

    def from_next(kind, cond, rel):
        q = where[rel]
        for window, at, _ in windows(q, core):
            pl.when(cond & window)(remote(
                grid.at[(1 - kind) * (last + 1), at], grid.at[(1 - kind) * (last + 1), at],
                plane_send_sem.at[0, 0], plane_recv_sem.at[kind, q // 2], core_to=1 - core,
            ).wait_recv)
        pl.when(cond & is_end(q, core) & has_beside)(halo(kind).wait_recv)

    for copies in loads[1:]:
        for copy in copies:
            copy.wait()

    theirs = pl.ds(1 + (1 - core) * planes, planes)

    def swap(step, rel, k, which):
        return [
            (cond, remote(
                grid.at[which, at], grid.at[which, at], pair_send_sem.at[step], pair_recv_sem.at[step], core_to=1 - core
            ))
            for cond, at, _ in windows(where[rel], k)
        ]

    def swapped(step, rel):
        for cond, copy in swap(step, rel, core, theirs):
            pl.when(cond)(copy.wait_recv)

    for k, (have, row, t) in enumerate(((has_high, rows, tile + 1), (has_low, 1, tile - 1))):
        begin(have, remote(
            grid.at[mine, row], grid.at[mine, k * (rows + 1)], edge_send_sem.at[k], edge_recv_sem.at[core],
            core_to=k, tile_to=t,
        ))
    for step, rel in enumerate(order):
        for cond, copy in swap(step, rel, 1 - core, mine):
            begin(cond, copy)

    for rel in odds:
        for k in range(2):
            planes_out(rel, k)

    def edges(cond):
        for k in range(2):
            which = pl.ds(1 + k * planes, planes)
            copy = remote(
                grid.at[which, far], grid.at[which, far], edge_send_sem.at[0], edge_recv_sem.at[k], core_to=1 - core
            )
            pl.when(cond & has_beside)(copy.wait_recv)

    lane = lax.broadcasted_iota(jnp.int32, (group, SUB, LANE), 2)
    sub = lax.broadcasted_iota(jnp.int32, (group, SUB, LANE), 1)
    left_edge = lane == 0
    right_edge = lane == LANE - 1
    left_end = left_edge & (sub == 0)
    right_end = right_edge & (sub == SUB - 1)
    scale = spacing * LOG2E

    def window(row):
        return pl.ds(row, group + 2)

    def plane_step(p, row, state):
        red, blue, green, through = state
        here = grid[p, window(row)]
        there = grid[p + 1, window(row)]
        total = here + there
        twice = total[1:-1]
        d_depth = there[1:-1] - here[1:-1]
        d_rows = total[2:] - total[:-2]
        from_left = pltpu.roll(twice, 1, 2)
        from_left = jnp.where(left_edge, pltpu.roll(from_left, 1, 1), from_left)
        from_left = jnp.where(left_end, 0.0, from_left)
        from_right = pltpu.roll(twice, LANE - 1, 2)
        from_right = jnp.where(right_edge, pltpu.roll(from_right, SUB - 1, 1), from_right)
        from_right = jnp.where(right_end, 0.0, from_right)
        d_cols = from_right - from_left
        facing = (0.25 * light_cols) * d_cols + (0.25 * light_rows) * d_rows + light_depth * d_depth
        length = (d_cols * d_cols + d_rows * d_rows) * 0.0625 + (d_depth * d_depth + 1.0)
        shading = 0.3 + 0.7 * jnp.abs(facing) * lax.rsqrt(length)
        optics = scale * floor_density
        for centre, width, bump in zip(centres, spreads, heights):
            root = math.sqrt(LOG2E) / width
            scaled = (0.5 * root) * twice - root * centre
            optics = optics + jnp.exp2(math.log2(bump * scale) - scaled * scaled)
        after = through * jnp.exp2(-optics)
        lit = (through - after) * shading
        middle = jnp.exp2((twice * (-0.25 * LOG2E)) * twice)
        balance = jnp.tanh(0.5 * twice)
        return (red + lit, blue + lit * balance, green + lit * middle, after)

    zero = jnp.zeros((group, SUB, LANE), jnp.float32)
    clear = (zero, zero, zero, zero + 1.0)
    def get(rel, at):
        return tuple(own[rel, c, at] for c in range(4))

    def put(rel, at, state):
        for c in range(4):
            own[rel, c, at] = state[c]

    def place(rel, i):
        turn = count(is_end(where[rel], core) & (core == 0))
        offset = (i + turn) % groups * group
        return pl.ds(offset, group), where[rel] * block + core * share + offset

    def near_state(row):
        state = clear
        for p in range(planes - 1):
            state = plane_step(1 + core * planes + p, row, state)
        return state

    def near_part(rel, low, high):
        def body(i, carry):
            at, row = place(rel, i)
            put(rel, at, near_state(row))
            return carry

        lax.fori_loop(low, high, body, 0)

    def compose(nearer, here, there):
        through = jnp.where(nearer, here[3], there[3])
        state = [
            jnp.where(nearer, here[c], there[c]) + through * jnp.where(nearer, there[c], here[c]) for c in range(3)
        ]
        return (*state, here[3] * there[3])

    def far_part(rel, low, high, both):
        def body(i, carry):
            at, row = place(rel, i)
            here = near_state(row) if both else get(rel, at)
            state = clear
            for p in range(planes):
                state = plane_step(planes - (planes - 1) * core + p, row, state)
            put(rel, at, compose(core == 0, here, state))
            return carry

        lax.fori_loop(low, high, body, 0)

    def in_front(rel):
        start = where[rel] * block + core * share

        @pl.when(has_front)
        def _():
            from_next(1, has_front, rel)

            def body(i, carry):
                at = pl.ds(i * group, group)
                red, blue, green, through = get(rel, at)
                first = plane_step(0, start + i * group, clear)
                put(rel, at, (
                    first[0] + first[3] * red, first[1] + first[3] * blue, first[2] + first[3] * green,
                    first[3] * through,
                ))
                return carry

            lax.fori_loop(0, groups, body, 0)

    def behind(rel, cond, low=0, high=groups):
        @pl.when(cond)
        def _():
            def body(i, carry):
                at, row = place(rel, i)
                put(rel, at, plane_step(last, row, get(rel, at)))
                return carry

            lax.fori_loop(low, high, body, 0)

    piece_copies = {}

    def forward(s, rel, i):
        j = rel >> (s + 1)
        slot = chips - (chips >> s) + j
        at, _ = place(rel, i)
        copy = remote(
            own.at[rel, :, at], pieces.at[slot, :, at], piece_send_sem.at[slot, i], piece_recv_sem.at[slot, i],
            opposite[s],
        )
        copy.start()
        piece_copies[s, j, i] = (copy, slot)

    for rel in order[:AHEAD]:
        near_part(rel, 0, groups - 1)
    def complete(step, rel, low, high):
        if low == high:
            return
        middle = min(high, groups - 1) if step < AHEAD else low
        if low < middle:
            far_part(rel, low, middle, False)
        if middle < high:
            far_part(rel, middle, high, True)
        if rel % 2:
            behind(rel, jnp.logical_not(has_behind), low, high)
            for i in range(low, high):
                forward(0, rel, i)

    swapped(0, order[0])
    for rel in odds:
        pass_on(rel)
    edges(always)
    for kind in range(2):
        begin(has_next[kind] & has_beside & ((chip + core) % 2 == 1), halo(kind))
    complete(0, order[0], 0, groups)
    for step, rel in enumerate(order[1:], 1):
        swapped(step, rel)
        complete(step, rel, 0, groups)

    def interfaces(rel):
        in_front(rel)
        from_next(0, has_behind, rel)
        behind(rel, always)

    for s in range(stages):
        nearer = chip // 2**s % 2 == 0
        for j in reversed(range(chips >> (s + 1))):
            rel = j << (s + 1)
            if s == 0:
                interfaces(rel)
            if s == stages - 1 or j == 0:
                drain()
            for i in range(groups):
                at, _ = place(rel, i)
                copy, slot = piece_copies[s, j, i]
                copy.wait_recv()
                state = compose(nearer, get(rel, at), [pieces[slot, c, at] for c in range(4)])
                if s < stages - 1:
                    put(rel, at, state)
                    if j % 2:
                        forward(s + 1, rel, i)
                else:
                    image = (0.5 * (state[0] + state[1]), state[2], 0.5 * (state[0] - state[1]), 1.0 - state[3])
                    for c in range(4):
                        result[at, c * SUB : (c + 1) * SUB, :] = image[c]
                    for b in range(cols // LANE):
                        out[at, :, b * LANE : (b + 1) * LANE] = result[at, pl.ds(b, 4, stride=SUB), :]

    for copy, _ in piece_copies.values():
        copy.wait_send()


def local(field):
    planes, rows, cols = field.shape
    depth_count = lax.axis_size("depth")
    chips = depth_count // 2
    share = rows // depth_count
    f32 = jnp.float32
    groups = min(share // g for g in range(1, 5) if share % g == 0)
    dims = (planes, rows, cols, depth_count, lax.axis_size("tile"), groups)
    dma = pltpu.SemaphoreType.DMA
    image = pl.pallas_call(
        functools.partial(kernel, dims),
        out_shape=jax.ShapeDtypeStruct((share, 4, cols), f32),
        in_specs=[pl.BlockSpec(memory_space=pltpu.HBM)],
        out_specs=pl.BlockSpec(memory_space=pltpu.VMEM),
        scratch_shapes=[
            pltpu.VMEM((2 * planes + 2, rows + 2, SUB, LANE), f32),
            pltpu.VMEM((chips, 4, share, SUB, LANE), f32),
            pltpu.VMEM((chips - 1, 4, share, SUB, LANE), f32),
            pltpu.VMEM((2, chips // 2, share + 2, SUB, LANE), f32),
            pltpu.VMEM((share, 4 * SUB, LANE), f32),
            dma((2, cols // LANE)),
            dma((chips,)),
            dma((chips,)),
            dma((2,)),
            dma((2,)),
            dma((2, chips // 2)),
            dma((2, chips // 2)),
            dma((2, chips // 2)),
            dma((2, chips // 2)),
            dma((2,)),
            dma((2,)),
            dma((chips - 1, groups)),
            dma((chips - 1, groups)),
        ],
        compiler_params=pltpu.CompilerParams(
            collective_id=0, has_side_effects=True, vmem_limit_bytes=55_000_000
        ),
    )(field)
    return jnp.transpose(image, (1, 0, 2))


def solution(mesh):
    return jax.shard_map(
        local,
        mesh=mesh,
        in_specs=(P("depth", "tile", None),),
        out_specs=P(None, ("tile", "depth"), None),
        check_vma=False,
    )
```

```python
import functools
import math

import jax
import jax.numpy as jnp
from jax import lax
from jax.experimental import pallas as pl
from jax.experimental.pallas import tpu as pltpu
from jax.sharding import PartitionSpec as P

centres = (-1.2, 0.3, 1.5)
spreads = (0.25, 0.35, 0.3)
heights = (2.0, 1.0, 3.0)
floor_density = 0.05
light_cols = 0.48
light_rows = 0.6
light_depth = 0.64

LOG2E = math.log2(math.e)
SUB, LANE = 8, 128
RELAY = ((3,), (3,))
AHEAD = 4


def kernel(
    dims, field, out, grid, own, pieces, passing, result,
    load_sem, pair_send_sem, pair_recv_sem, edge_send_sem, edge_recv_sem,
    plane_send_sem, plane_recv_sem, passing_send_sem, passing_recv_sem, halo_send_sem, halo_recv_sem,
    piece_send_sem, piece_recv_sem,
):
    planes, rows, cols, depth_count, tile_count, groups = dims
    chips = depth_count // 2
    share = rows // depth_count
    block = 2 * share
    spacing = 3.0 / (planes * depth_count)
    group = share // groups
    me = lax.axis_index("depth")
    tile = lax.axis_index("tile")
    chip = me // 2
    core = me % 2
    stages = chips.bit_length() - 1
    assert chips == 1 << stages
    order = sorted(range(1, chips), key=lambda rel: (rel & -rel, -rel)) + [0]
    last = 2 * planes
    mine = pl.ds(1 + core * planes, planes)

    def relative(base, rel):
        for s in range(stages):
            if rel >> s & 1:
                base = base + (1 - 2 * (base // 2**s % 2)) * 2**s
        return base

    def remote(src, dst, send_sem, recv_sem, chip_to=chip, core_to=core, tile_to=tile):
        return pltpu.make_async_remote_copy(
            src_ref=src, dst_ref=dst, send_sem=send_sem, recv_sem=recv_sem,
            device_id=(chip_to * 2 + core_to, tile_to), device_id_type=pl.DeviceIdType.MESH,
        )

    has_front = chip > 0
    has_behind = chip < chips - 1
    has_low = tile > 0
    has_high = tile < tile_count - 1
    opposite = [relative(chip, 1 << s) for s in range(stages)]
    odd = chip % 2
    has_far = jnp.where(odd == 0, has_front, has_behind)
    far_chip = jnp.where(has_far, chip - 1 + 2 * odd, chip)

    barrier = pltpu.get_barrier_semaphore()

    def greet(cond, c, k, t):
        @pl.when(cond)
        def _():
            pl.semaphore_signal(barrier, inc=1, device_id=(c * 2 + k, t), device_id_type=pl.DeviceIdType.MESH)

    always = chip >= 0
    has_beside = jnp.where(core == 0, has_low, has_high)
    beside = tile - 1 + 2 * core
    far = core * (rows + 1)
    greet(has_beside, chip, 0, beside)
    greet(has_beside, chip, 1, beside)
    greet(has_far & (core == odd), far_chip, 1 - core, tile)
    greet(has_far, far_chip, core, tile)
    greet(always, opposite[0], 1 - core, tile)
    for c in opposite:
        greet(always, c, core, tile)
    greet(always, chip, 1 - core, tile)

    def count(cond):
        return cond.astype(jnp.int32)

    blank = jnp.zeros((SUB, LANE), jnp.float32)

    def load(p, count, k):
        return [
            pltpu.make_async_copy(
                field.at[pl.ds(p, count), :, pl.ds(j * LANE, LANE)],
                grid.at[pl.ds(1 + core * planes + p, count), pl.ds(1, rows), j, :],
                load_sem.at[k, j],
            )
            for j in range(cols // LANE)
        ]

    loads = [load(core * (planes - 1), 1, 0), load(1 - core, planes - 1, 1)]
    for copies in loads:
        for copy in copies:
            copy.start()

    @pl.when(jnp.logical_not(has_beside))
    def _():
        for p in range(last + 2):
            grid[p, far] = blank

    @pl.when(jnp.logical_not(has_behind))
    def _():
        grid[last + 1] = jnp.zeros(grid.shape[1:], jnp.float32)

    for copy in loads[0]:
        copy.wait()
    pl.semaphore_wait(barrier, 2 + stages + count(has_far) + count(has_far & (core == odd)) + count(has_low) + count(has_high))

    sent = []

    def begin(cond, copy):
        if cond is always:
            copy.start()
        else:
            pl.when(cond)(copy.start)
        sent.append((cond, copy))

    def drain():
        for cond, copy in sent:
            if cond is always:
                copy.wait_send()
            else:
                pl.when(cond)(copy.wait_send)
        sent.clear()

    def is_end(q, k):
        return jnp.where(k == 0, q == 0, q == chips - 1)

    evens = range(0, chips, 2)
    next_chip = [jnp.where(has_front, chip - 1, chip), jnp.where(has_behind, chip + 1, chip)]
    has_next = [has_front, has_behind]

    where = [relative(chip, rel) for rel in range(chips)]
    odds = [rel for rel in order if rel % 2]

    def windows(q, k):
        start = q * block + k * share
        end = is_end(q, k)
        skip = count(start == 0)
        return [
            (jnp.logical_not(end), pl.ds(start, share + 2), pl.ds(0, share + 2)),
            (end, pl.ds(start + skip, share + 1), pl.ds(skip, share + 1)),
        ]

    from_plane = 1 + core * (last - 1)
    to_plane = (1 - core) * (last + 1)
    meets = jnp.where(core == 0, next_chip[0], next_chip[1])
    has_meets = jnp.where(core == 0, has_front, has_behind)
    quarter = chip % 4
    def turns(rel, k):
        if stages < 2 or rel % 2 == 0:
            return chip < 0
        return always if rel % 4 in RELAY[0] and rel % 4 in RELAY[1] else (
            k == 0 if rel % 4 in RELAY[0] else k == 1 if rel % 4 in RELAY[1] else chip < 0
        )


    def planes_out(rel, k):
        q = where[rel]
        around = (quarter == 2 - core) & has_meets & turns(rel, core)
        due = has_meets & jnp.logical_not(around)
        if rel == 1 and k == 1:
            due = due & jnp.logical_not((odd == 1) & (core == 0))
        if rel == 0:
            due = due & (odd == 0) & (core == 1)
        slot = rel // 2
        for cond, at, local_at in windows(q, k):
            if rel % 2:
                begin(cond & around, remote(
                    grid.at[from_plane, at], passing.at[k, slot, local_at],
                    plane_send_sem.at[k, rel], passing_recv_sem.at[k, slot], opposite[1],
                ))
            begin(cond & due, remote(
                grid.at[from_plane, at], grid.at[to_plane, at],
                plane_send_sem.at[k, rel], plane_recv_sem.at[core, q], meets, k,
            ))

    def pass_on(rel):
        slot = rel // 2
        q = relative(opposite[1], rel)
        for k in range(2):
            for cond, at, local_at in windows(q, k):
                cond = cond & (quarter == 3 * core) & turns(rel, core)
                arriving = remote(
                    passing.at[k, slot, local_at], passing.at[k, slot, local_at],
                    passing_send_sem.at[k, slot], passing_recv_sem.at[k, slot], opposite[1],
                )
                pl.when(cond)(arriving.wait_recv)
                begin(cond, remote(
                    passing.at[k, slot, local_at], grid.at[to_plane, at],
                    passing_send_sem.at[k, slot], plane_recv_sem.at[core, q], opposite[0], k,
                ))

    def halo(kind):
        return remote(
            grid.at[1 + kind * (last - 1), far], grid.at[(1 - kind) * (last + 1), far],
            halo_send_sem.at[kind], halo_recv_sem.at[kind], next_chip[kind],
        )

    def from_next(kind, cond, rel):
        q = where[rel]
        for window, at, _ in windows(q, core):
            pl.when(cond & window)(remote(
                grid.at[(1 - kind) * (last + 1), at], grid.at[(1 - kind) * (last + 1), at],
                plane_send_sem.at[0, 0], plane_recv_sem.at[kind, q], core_to=1 - core,
            ).wait_recv)
        pl.when(cond & is_end(q, core) & has_beside)(halo(kind).wait_recv)

    planes_out(0, 1)
    for rel in odds:
        for k in range(2):
            planes_out(rel, k)

    for copies in loads[1:]:
        for copy in copies:
            copy.wait()

    theirs = pl.ds(1 + (1 - core) * planes, planes)

    def swap(step, rel, k, which):
        return [
            (cond, remote(
                grid.at[which, at], grid.at[which, at], pair_send_sem.at[step], pair_recv_sem.at[step], core_to=1 - core
            ))
            for cond, at, _ in windows(where[rel], k)
        ]

    def swapped(step, rel):
        for cond, copy in swap(step, rel, core, theirs):
            pl.when(cond)(copy.wait_recv)

    for step, rel in enumerate(order):
        for cond, copy in swap(step, rel, 1 - core, mine):
            begin(cond, copy)
        if step == 0:
            for k, (have, row, t) in enumerate(((has_high, rows, tile + 1), (has_low, 1, tile - 1))):
                begin(have, remote(
                    grid.at[mine, row], grid.at[mine, k * (rows + 1)], edge_send_sem.at[k], edge_recv_sem.at[core],
                    core_to=k, tile_to=t,
                ))

    def edges(cond):
        for k in range(2):
            which = pl.ds(1 + k * planes, planes)
            copy = remote(
                grid.at[which, far], grid.at[which, far], edge_send_sem.at[0], edge_recv_sem.at[k], core_to=1 - core
            )
            pl.when(cond & has_beside)(copy.wait_recv)

    lane = lax.broadcasted_iota(jnp.int32, (group, SUB, LANE), 2)
    sub = lax.broadcasted_iota(jnp.int32, (group, SUB, LANE), 1)
    left_edge = lane == 0
    right_edge = lane == LANE - 1
    left_end = left_edge & (sub == 0)
    right_end = right_edge & (sub == SUB - 1)
    scale = spacing * LOG2E

    def window(row):
        return pl.ds(row, group + 2)

    def plane_step(p, row, state):
        red, blue, green, through = state
        here = grid[p, window(row)]
        there = grid[p + 1, window(row)]
        total = here + there
        twice = total[1:-1]
        d_depth = there[1:-1] - here[1:-1]
        d_rows = total[2:] - total[:-2]
        from_left = pltpu.roll(twice, 1, 2)
        from_left = jnp.where(left_edge, pltpu.roll(from_left, 1, 1), from_left)
        from_left = jnp.where(left_end, 0.0, from_left)
        from_right = pltpu.roll(twice, LANE - 1, 2)
        from_right = jnp.where(right_edge, pltpu.roll(from_right, SUB - 1, 1), from_right)
        from_right = jnp.where(right_end, 0.0, from_right)
        d_cols = from_right - from_left
        facing = (0.25 * light_cols) * d_cols + (0.25 * light_rows) * d_rows + light_depth * d_depth
        length = (d_cols * d_cols + d_rows * d_rows) * 0.0625 + (d_depth * d_depth + 1.0)
        shading = 0.3 + 0.7 * jnp.abs(facing) * lax.rsqrt(length)
        optics = scale * floor_density
        for centre, width, bump in zip(centres, spreads, heights):
            root = math.sqrt(LOG2E) / width
            scaled = (0.5 * root) * twice - root * centre
            optics = optics + jnp.exp2(math.log2(bump * scale) - scaled * scaled)
        after = through * jnp.exp2(-optics)
        lit = (through - after) * shading
        middle = jnp.exp2((twice * (-0.25 * LOG2E)) * twice)
        balance = jnp.tanh(0.5 * twice)
        return (red + lit, blue + lit * balance, green + lit * middle, after)

    zero = jnp.zeros((group, SUB, LANE), jnp.float32)
    clear = (zero, zero, zero, zero + 1.0)
    def get(rel, at):
        return tuple(own[rel, c, at] for c in range(4))

    def put(rel, at, state):
        for c in range(4):
            own[rel, c, at] = state[c]

    def place(rel, i):
        turn = count(is_end(where[rel], core) & (core == 0))
        offset = (i + turn) % groups * group
        return pl.ds(offset, group), where[rel] * block + core * share + offset

    def near_state(row):
        state = clear
        for p in range(planes - 1):
            state = plane_step(1 + core * planes + p, row, state)
        return state

    def near_part(rel, low, high):
        def body(i, carry):
            at, row = place(rel, i)
            put(rel, at, near_state(row))
            return carry

        lax.fori_loop(low, high, body, 0)

    def compose(nearer, here, there):
        through = jnp.where(nearer, here[3], there[3])
        state = [
            jnp.where(nearer, here[c], there[c]) + through * jnp.where(nearer, there[c], here[c]) for c in range(3)
        ]
        return (*state, here[3] * there[3])

    def far_part(rel, low, high, both):
        def body(i, carry):
            at, row = place(rel, i)
            here = near_state(row) if both else get(rel, at)
            state = clear
            for p in range(planes):
                state = plane_step(planes - (planes - 1) * core + p, row, state)
            put(rel, at, compose(core == 0, here, state))
            return carry

        lax.fori_loop(low, high, body, 0)

    def in_front(rel, cond):
        start = where[rel] * block + core * share

        @pl.when(cond)
        def _():
            from_next(1, has_front, rel)

            def body(i, carry):
                at = pl.ds(i * group, group)
                red, blue, green, through = get(rel, at)
                first = plane_step(0, start + i * group, clear)
                put(rel, at, (
                    first[0] + first[3] * red, first[1] + first[3] * blue, first[2] + first[3] * green,
                    first[3] * through,
                ))
                return carry

            lax.fori_loop(0, groups, body, 0)

    def behind(rel, cond, low=0, high=groups):
        @pl.when(cond)
        def _():
            def body(i, carry):
                at, row = place(rel, i)
                put(rel, at, plane_step(last, row, get(rel, at)))
                return carry

            lax.fori_loop(low, high, body, 0)

    piece_copies = {}

    def forward(s, rel, i):
        j = rel >> (s + 1)
        slot = chips - (chips >> s) + j
        at, _ = place(rel, i)
        copy = remote(
            own.at[rel, :, at], pieces.at[slot, :, at], piece_send_sem.at[slot, i], piece_recv_sem.at[slot, i],
            opposite[s],
        )
        copy.start()
        piece_copies[s, j, i] = (copy, slot)

    for rel in order[:AHEAD]:
        near_part(rel, 0, groups - 1)
    def complete(step, rel, low, high):
        if low == high:
            return
        middle = min(high, groups - 1) if step < AHEAD else low
        if low < middle:
            far_part(rel, low, middle, False)
        if middle < high:
            far_part(rel, middle, high, True)
        if rel % 2:
            if rel == 1 and high == groups:
                in_front(rel, (odd == 1) & (core == 1))
            behind(rel, jnp.logical_not(has_behind), low, high)
            for i in range(low, high):
                forward(0, rel, i)

    swapped(0, order[0])
    for rel in odds:
        pass_on(rel)
    edges(always)
    for kind in range(2):
        begin(has_next[kind] & has_beside & ((chip + core) % 2 == 1), halo(kind))
    complete(0, order[0], 0, groups)
    for step, rel in enumerate(order[1:], 1):
        swapped(step, rel)
        complete(step, rel, 0, groups)

    def interfaces(rel):
        in_front(rel, has_front)
        if rel == 0:
            from_next(0, has_behind & ((odd == 1) | (core == 0)), rel)
            behind(rel, (odd == 1) | (core == 0))
        else:
            from_next(0, has_behind, rel)
            behind(rel, always)

    for s in range(stages):
        nearer = chip // 2**s % 2 == 0
        for j in reversed(range(chips >> (s + 1))):
            rel = j << (s + 1)
            if s == 0:
                interfaces(rel)
            if s == stages - 1 or j == 0:
                drain()
            for i in range(groups):
                at, _ = place(rel, i)
                copy, slot = piece_copies[s, j, i]
                copy.wait_recv()
                state = compose(nearer, get(rel, at), [pieces[slot, c, at] for c in range(4)])
                if s < stages - 1:
                    put(rel, at, state)
                    if j % 2:
                        forward(s + 1, rel, i)
                else:
                    image = (0.5 * (state[0] + state[1]), state[2], 0.5 * (state[0] - state[1]), 1.0 - state[3])
                    for c in range(4):
                        result[at, c * SUB : (c + 1) * SUB, :] = image[c]
                    for b in range(cols // LANE):
                        out[at, :, b * LANE : (b + 1) * LANE] = result[at, pl.ds(b, 4, stride=SUB), :]

    for copy, _ in piece_copies.values():
        copy.wait_send()


def local(field):
    planes, rows, cols = field.shape
    depth_count = lax.axis_size("depth")
    chips = depth_count // 2
    share = rows // depth_count
    f32 = jnp.float32
    groups = min(share // g for g in range(1, 5) if share % g == 0)
    dims = (planes, rows, cols, depth_count, lax.axis_size("tile"), groups)
    dma = pltpu.SemaphoreType.DMA
    image = pl.pallas_call(
        functools.partial(kernel, dims),
        out_shape=jax.ShapeDtypeStruct((share, 4, cols), f32),
        in_specs=[pl.BlockSpec(memory_space=pltpu.HBM)],
        out_specs=pl.BlockSpec(memory_space=pltpu.VMEM),
        scratch_shapes=[
            pltpu.VMEM((2 * planes + 2, rows + 2, SUB, LANE), f32),
            pltpu.VMEM((chips, 4, share, SUB, LANE), f32),
            pltpu.VMEM((chips - 1, 4, share, SUB, LANE), f32),
            pltpu.VMEM((2, chips // 2, share + 2, SUB, LANE), f32),
            pltpu.VMEM((share, 4 * SUB, LANE), f32),
            dma((2, cols // LANE)),
            dma((chips,)),
            dma((chips,)),
            dma((2,)),
            dma((2,)),
            dma((2, chips)),
            dma((2, chips)),
            dma((2, chips // 2)),
            dma((2, chips // 2)),
            dma((2,)),
            dma((2,)),
            dma((chips - 1, groups)),
            dma((chips - 1, groups)),
        ],
        compiler_params=pltpu.CompilerParams(
            collective_id=0, has_side_effects=True, vmem_limit_bytes=55_000_000
        ),
    )(field)
    return jnp.transpose(image, (1, 0, 2))


def solution(mesh):
    return jax.shard_map(
        local,
        mesh=mesh,
        in_specs=(P("depth", "tile", None),),
        out_specs=P(None, ("tile", "depth"), None),
        check_vma=False,
    )
```

```python
import functools
import math

import jax
import jax.numpy as jnp
from jax import lax
from jax.experimental import pallas as pl
from jax.experimental.pallas import tpu as pltpu
from jax.sharding import PartitionSpec as P

centres = (-1.2, 0.3, 1.5)
spreads = (0.25, 0.35, 0.3)
heights = (2.0, 1.0, 3.0)
floor_density = 0.05
light_cols = 0.48
light_rows = 0.6
light_depth = 0.64

LOG2E = math.log2(math.e)
SUB, LANE = 8, 128
RELAY = ((3,), (3,))
AHEAD = 4


def kernel(
    dims, field, out, grid, own, pieces, passing, result,
    load_sem, pair_send_sem, pair_recv_sem, edge_send_sem, edge_recv_sem,
    plane_send_sem, plane_recv_sem, passing_send_sem, passing_recv_sem, halo_send_sem, halo_recv_sem,
    piece_send_sem, piece_recv_sem,
):
    planes, rows, cols, depth_count, tile_count, groups = dims
    chips = depth_count // 2
    share = rows // depth_count
    block = 2 * share
    spacing = 3.0 / (planes * depth_count)
    group = share // groups
    me = lax.axis_index("depth")
    tile = lax.axis_index("tile")
    chip = me // 2
    core = me % 2
    stages = chips.bit_length() - 1
    assert chips == 1 << stages
    order = sorted(range(1, chips), key=lambda rel: (rel & -rel, -rel)) + [0]
    last = 2 * planes
    mine = pl.ds(1 + core * planes, planes)

    def relative(base, rel):
        for s in range(stages):
            if rel >> s & 1:
                base = base + (1 - 2 * (base // 2**s % 2)) * 2**s
        return base

    def remote(src, dst, send_sem, recv_sem, chip_to=chip, core_to=core, tile_to=tile):
        return pltpu.make_async_remote_copy(
            src_ref=src, dst_ref=dst, send_sem=send_sem, recv_sem=recv_sem,
            device_id=(chip_to * 2 + core_to, tile_to), device_id_type=pl.DeviceIdType.MESH,
        )

    has_front = chip > 0
    has_behind = chip < chips - 1
    has_low = tile > 0
    has_high = tile < tile_count - 1
    opposite = [relative(chip, 1 << s) for s in range(stages)]
    odd = chip % 2
    has_far = jnp.where(odd == 0, has_front, has_behind)
    far_chip = jnp.where(has_far, chip - 1 + 2 * odd, chip)

    barrier = pltpu.get_barrier_semaphore()

    def greet(cond, c, k, t):
        @pl.when(cond)
        def _():
            pl.semaphore_signal(barrier, inc=1, device_id=(c * 2 + k, t), device_id_type=pl.DeviceIdType.MESH)

    always = chip >= 0
    has_beside = jnp.where(core == 0, has_low, has_high)
    beside = tile - 1 + 2 * core
    far = core * (rows + 1)
    greet(has_beside, chip, 0, beside)
    greet(has_beside, chip, 1, beside)
    greet(has_far & (core == odd), far_chip, 1 - core, tile)
    greet(has_far, far_chip, core, tile)
    greet(always, opposite[0], 1 - core, tile)
    for c in opposite:
        greet(always, c, core, tile)
    greet(always, chip, 1 - core, tile)

    def count(cond):
        return cond.astype(jnp.int32)

    blank = jnp.zeros((SUB, LANE), jnp.float32)

    def load(p, count, k):
        return [
            pltpu.make_async_copy(
                field.at[pl.ds(p, count), :, pl.ds(j * LANE, LANE)],
                grid.at[pl.ds(1 + core * planes + p, count), pl.ds(1, rows), j, :],
                load_sem.at[k, j],
            )
            for j in range(cols // LANE)
        ]

    loads = [load(core * (planes - 1), 1, 0), load(1 - core, planes - 1, 1)]
    for copies in loads:
        for copy in copies:
            copy.start()

    @pl.when(jnp.logical_not(has_beside))
    def _():
        for p in range(last + 2):
            grid[p, far] = blank

    @pl.when(jnp.logical_not(has_behind))
    def _():
        grid[last + 1] = jnp.zeros(grid.shape[1:], jnp.float32)

    for copy in loads[0]:
        copy.wait()
    pl.semaphore_wait(barrier, 2 + stages + count(has_far) + count(has_far & (core == odd)) + count(has_low) + count(has_high))

    sent = []

    def begin(cond, copy):
        if cond is always:
            copy.start()
        else:
            pl.when(cond)(copy.start)
        sent.append((cond, copy))

    def drain():
        for cond, copy in sent:
            if cond is always:
                copy.wait_send()
            else:
                pl.when(cond)(copy.wait_send)
        sent.clear()

    def is_end(q, k):
        return jnp.where(k == 0, q == 0, q == chips - 1)

    evens = range(0, chips, 2)
    next_chip = [jnp.where(has_front, chip - 1, chip), jnp.where(has_behind, chip + 1, chip)]
    has_next = [has_front, has_behind]

    where = [relative(chip, rel) for rel in range(chips)]
    odds = [rel for rel in order if rel % 2]

    def windows(q, k):
        start = q * block + k * share
        end = is_end(q, k)
        skip = count(start == 0)
        return [
            (jnp.logical_not(end), pl.ds(start, share + 2), pl.ds(0, share + 2)),
            (end, pl.ds(start + skip, share + 1), pl.ds(skip, share + 1)),
        ]

    from_plane = 1 + core * (last - 1)
    to_plane = (1 - core) * (last + 1)
    meets = jnp.where(core == 0, next_chip[0], next_chip[1])
    has_meets = jnp.where(core == 0, has_front, has_behind)
    quarter = chip % 4
    def turns(rel, k):
        if stages < 2 or rel % 2 == 0:
            return chip < 0
        return always if rel % 4 in RELAY[0] and rel % 4 in RELAY[1] else (
            k == 0 if rel % 4 in RELAY[0] else k == 1 if rel % 4 in RELAY[1] else chip < 0
        )


    def planes_out(rel, k):
        q = where[rel]
        around = (quarter == 2 - core) & has_meets & turns(rel, core)
        due = has_meets & jnp.logical_not(around)
        if rel == 1 and k == 1:
            due = due & jnp.logical_not((odd == 1) & (core == 0))
        if rel == 0:
            due = due & (odd == 0) & (core == 1)
        slot = rel // 2
        for cond, at, local_at in windows(q, k):
            if rel % 2:
                begin(cond & around, remote(
                    grid.at[from_plane, at], passing.at[k, slot, local_at],
                    plane_send_sem.at[k, rel], passing_recv_sem.at[k, slot], opposite[1],
                ))
            begin(cond & due, remote(
                grid.at[from_plane, at], grid.at[to_plane, at],
                plane_send_sem.at[k, rel], plane_recv_sem.at[core, q], meets, k,
            ))

    def pass_on(rel):
        slot = rel // 2
        q = relative(opposite[1], rel)
        for k in range(2):
            for cond, at, local_at in windows(q, k):
                cond = cond & (quarter == 3 * core) & turns(rel, core)
                arriving = remote(
                    passing.at[k, slot, local_at], passing.at[k, slot, local_at],
                    passing_send_sem.at[k, slot], passing_recv_sem.at[k, slot], opposite[1],
                )
                pl.when(cond)(arriving.wait_recv)
                begin(cond, remote(
                    passing.at[k, slot, local_at], grid.at[to_plane, at],
                    passing_send_sem.at[k, slot], plane_recv_sem.at[core, q], opposite[0], k,
                ))

    def halo(kind):
        return remote(
            grid.at[1 + kind * (last - 1), far], grid.at[(1 - kind) * (last + 1), far],
            halo_send_sem.at[kind], halo_recv_sem.at[kind], next_chip[kind],
        )

    def from_next(kind, cond, rel):
        q = where[rel]
        for window, at, _ in windows(q, core):
            pl.when(cond & window)(remote(
                grid.at[(1 - kind) * (last + 1), at], grid.at[(1 - kind) * (last + 1), at],
                plane_send_sem.at[0, 0], plane_recv_sem.at[kind, q], core_to=1 - core,
            ).wait_recv)
        pl.when(cond & is_end(q, core) & has_beside)(halo(kind).wait_recv)

    for copies in loads[1:]:
        for copy in copies:
            copy.wait()

    theirs = pl.ds(1 + (1 - core) * planes, planes)

    def swap(step, rel, k, which):
        return [
            (cond, remote(
                grid.at[which, at], grid.at[which, at], pair_send_sem.at[step], pair_recv_sem.at[step], core_to=1 - core
            ))
            for cond, at, _ in windows(where[rel], k)
        ]

    def swapped(step, rel):
        for cond, copy in swap(step, rel, core, theirs):
            pl.when(cond)(copy.wait_recv)

    for k, (have, row, t) in enumerate(((has_high, rows, tile + 1), (has_low, 1, tile - 1))):
        begin(have, remote(
            grid.at[mine, row], grid.at[mine, k * (rows + 1)], edge_send_sem.at[k], edge_recv_sem.at[core],
            core_to=k, tile_to=t,
        ))
    for step, rel in enumerate(order):
        for cond, copy in swap(step, rel, 1 - core, mine):
            begin(cond, copy)

    planes_out(0, 1)
    for rel in odds:
        for k in range(2):
            planes_out(rel, k)

    def edges(cond):
        for k in range(2):
            which = pl.ds(1 + k * planes, planes)
            copy = remote(
                grid.at[which, far], grid.at[which, far], edge_send_sem.at[0], edge_recv_sem.at[k], core_to=1 - core
            )
            pl.when(cond & has_beside)(copy.wait_recv)

    lane = lax.broadcasted_iota(jnp.int32, (group, SUB, LANE), 2)
    sub = lax.broadcasted_iota(jnp.int32, (group, SUB, LANE), 1)
    left_edge = lane == 0
    right_edge = lane == LANE - 1
    left_end = left_edge & (sub == 0)
    right_end = right_edge & (sub == SUB - 1)
    scale = spacing * LOG2E

    def window(row):
        return pl.ds(row, group + 2)

    def plane_step(p, row, state):
        red, blue, green, through = state
        here = grid[p, window(row)]
        there = grid[p + 1, window(row)]
        total = here + there
        twice = total[1:-1]
        d_depth = there[1:-1] - here[1:-1]
        d_rows = total[2:] - total[:-2]
        from_left = pltpu.roll(twice, 1, 2)
        from_left = jnp.where(left_edge, pltpu.roll(from_left, 1, 1), from_left)
        from_left = jnp.where(left_end, 0.0, from_left)
        from_right = pltpu.roll(twice, LANE - 1, 2)
        from_right = jnp.where(right_edge, pltpu.roll(from_right, SUB - 1, 1), from_right)
        from_right = jnp.where(right_end, 0.0, from_right)
        d_cols = from_right - from_left
        facing = (0.25 * light_cols) * d_cols + (0.25 * light_rows) * d_rows + light_depth * d_depth
        length = (d_cols * d_cols + d_rows * d_rows) * 0.0625 + (d_depth * d_depth + 1.0)
        shading = 0.3 + 0.7 * jnp.abs(facing) * lax.rsqrt(length)
        optics = scale * floor_density
        for centre, width, bump in zip(centres, spreads, heights):
            root = math.sqrt(LOG2E) / width
            scaled = (0.5 * root) * twice - root * centre
            optics = optics + jnp.exp2(math.log2(bump * scale) - scaled * scaled)
        after = through * jnp.exp2(-optics)
        lit = (through - after) * shading
        middle = jnp.exp2((twice * (-0.25 * LOG2E)) * twice)
        balance = jnp.tanh(0.5 * twice)
        return (red + lit, blue + lit * balance, green + lit * middle, after)

    zero = jnp.zeros((group, SUB, LANE), jnp.float32)
    clear = (zero, zero, zero, zero + 1.0)
    def get(rel, at):
        return tuple(own[rel, c, at] for c in range(4))

    def put(rel, at, state):
        for c in range(4):
            own[rel, c, at] = state[c]

    def place(rel, i):
        turn = count(is_end(where[rel], core) & (core == 0))
        offset = (i + turn) % groups * group
        return pl.ds(offset, group), where[rel] * block + core * share + offset

    def near_state(row):
        state = clear
        for p in range(planes - 1):
            state = plane_step(1 + core * planes + p, row, state)
        return state

    def near_part(rel, low, high):
        def body(i, carry):
            at, row = place(rel, i)
            put(rel, at, near_state(row))
            return carry

        lax.fori_loop(low, high, body, 0)

    def compose(nearer, here, there):
        through = jnp.where(nearer, here[3], there[3])
        state = [
            jnp.where(nearer, here[c], there[c]) + through * jnp.where(nearer, there[c], here[c]) for c in range(3)
        ]
        return (*state, here[3] * there[3])

    def far_part(rel, low, high, both):
        def body(i, carry):
            at, row = place(rel, i)
            here = near_state(row) if both else get(rel, at)
            state = clear
            for p in range(planes):
                state = plane_step(planes - (planes - 1) * core + p, row, state)
            put(rel, at, compose(core == 0, here, state))
            return carry

        lax.fori_loop(low, high, body, 0)

    def in_front(rel, cond):
        start = where[rel] * block + core * share

        @pl.when(cond)
        def _():
            from_next(1, has_front, rel)

            def body(i, carry):
                at = pl.ds(i * group, group)
                red, blue, green, through = get(rel, at)
                first = plane_step(0, start + i * group, clear)
                put(rel, at, (
                    first[0] + first[3] * red, first[1] + first[3] * blue, first[2] + first[3] * green,
                    first[3] * through,
                ))
                return carry

            lax.fori_loop(0, groups, body, 0)

    def behind(rel, cond, low=0, high=groups):
        @pl.when(cond)
        def _():
            def body(i, carry):
                at, row = place(rel, i)
                put(rel, at, plane_step(last, row, get(rel, at)))
                return carry

            lax.fori_loop(low, high, body, 0)

    piece_copies = {}

    def forward(s, rel, i):
        j = rel >> (s + 1)
        slot = chips - (chips >> s) + j
        at, _ = place(rel, i)
        copy = remote(
            own.at[rel, :, at], pieces.at[slot, :, at], piece_send_sem.at[slot, i], piece_recv_sem.at[slot, i],
            opposite[s],
        )
        copy.start()
        piece_copies[s, j, i] = (copy, slot)

    for rel in order[:AHEAD]:
        near_part(rel, 0, groups - 1)
    def complete(step, rel, low, high):
        if low == high:
            return
        middle = min(high, groups - 1) if step < AHEAD else low
        if low < middle:
            far_part(rel, low, middle, False)
        if middle < high:
            far_part(rel, middle, high, True)
        if rel % 2:
            if rel == 1 and high == groups:
                in_front(rel, (odd == 1) & (core == 1))
            behind(rel, jnp.logical_not(has_behind), low, high)
            for i in range(low, high):
                forward(0, rel, i)

    swapped(0, order[0])
    for rel in odds:
        pass_on(rel)
    far_part(order[0], 0, groups - 1, False)
    edges(always)
    for kind in range(2):
        begin(has_next[kind] & has_beside & ((chip + core) % 2 == 1), halo(kind))
    far_part(order[0], groups - 1, groups, True)
    behind(order[0], jnp.logical_not(has_behind))
    for i in range(groups):
        forward(0, order[0], i)
    for step, rel in enumerate(order[1:], 1):
        swapped(step, rel)
        complete(step, rel, 0, groups)

    def interfaces(rel):
        in_front(rel, has_front)
        if rel == 0:
            from_next(0, has_behind & ((odd == 1) | (core == 0)), rel)
            behind(rel, (odd == 1) | (core == 0))
        else:
            from_next(0, has_behind, rel)
            behind(rel, always)

    for s in range(stages):
        nearer = chip // 2**s % 2 == 0
        for j in reversed(range(chips >> (s + 1))):
            rel = j << (s + 1)
            if s == 0:
                interfaces(rel)
            if s == stages - 1 or j == 0:
                drain()
            for i in range(groups):
                at, _ = place(rel, i)
                copy, slot = piece_copies[s, j, i]
                copy.wait_recv()
                state = compose(nearer, get(rel, at), [pieces[slot, c, at] for c in range(4)])
                if s < stages - 1:
                    put(rel, at, state)
                    if j % 2:
                        forward(s + 1, rel, i)
                else:
                    image = (0.5 * (state[0] + state[1]), state[2], 0.5 * (state[0] - state[1]), 1.0 - state[3])
                    for c in range(4):
                        result[at, c * SUB : (c + 1) * SUB, :] = image[c]
                    for b in range(cols // LANE):
                        out[at, :, b * LANE : (b + 1) * LANE] = result[at, pl.ds(b, 4, stride=SUB), :]

    for copy, _ in piece_copies.values():
        copy.wait_send()


def local(field):
    planes, rows, cols = field.shape
    depth_count = lax.axis_size("depth")
    chips = depth_count // 2
    share = rows // depth_count
    f32 = jnp.float32
    groups = min(share // g for g in range(1, 5) if share % g == 0)
    dims = (planes, rows, cols, depth_count, lax.axis_size("tile"), groups)
    dma = pltpu.SemaphoreType.DMA
    image = pl.pallas_call(
        functools.partial(kernel, dims),
        out_shape=jax.ShapeDtypeStruct((share, 4, cols), f32),
        in_specs=[pl.BlockSpec(memory_space=pltpu.HBM)],
        out_specs=pl.BlockSpec(memory_space=pltpu.VMEM),
        scratch_shapes=[
            pltpu.VMEM((2 * planes + 2, rows + 2, SUB, LANE), f32),
            pltpu.VMEM((chips, 4, share, SUB, LANE), f32),
            pltpu.VMEM((chips - 1, 4, share, SUB, LANE), f32),
            pltpu.VMEM((2, chips // 2, share + 2, SUB, LANE), f32),
            pltpu.VMEM((share, 4 * SUB, LANE), f32),
            dma((2, cols // LANE)),
            dma((chips,)),
            dma((chips,)),
            dma((2,)),
            dma((2,)),
            dma((2, chips)),
            dma((2, chips)),
            dma((2, chips // 2)),
            dma((2, chips // 2)),
            dma((2,)),
            dma((2,)),
            dma((chips - 1, groups)),
            dma((chips - 1, groups)),
        ],
        compiler_params=pltpu.CompilerParams(
            collective_id=0, has_side_effects=True, vmem_limit_bytes=55_000_000
        ),
    )(field)
    return jnp.transpose(image, (1, 0, 2))


def solution(mesh):
    return jax.shard_map(
        local,
        mesh=mesh,
        in_specs=(P("depth", "tile", None),),
        out_specs=P(None, ("tile", "depth"), None),
        check_vma=False,
    )
```

```python
import functools
import math

import jax
import jax.numpy as jnp
from jax import lax
from jax.experimental import pallas as pl
from jax.experimental.pallas import tpu as pltpu
from jax.sharding import PartitionSpec as P

centres = (-1.2, 0.3, 1.5)
spreads = (0.25, 0.35, 0.3)
heights = (2.0, 1.0, 3.0)
floor_density = 0.05
light_cols = 0.48
light_rows = 0.6
light_depth = 0.64

LOG2E = math.log2(math.e)
SUB, LANE = 8, 128
RELAY = ((3,), (3,))
AHEAD = 4


def kernel(
    dims, field, out, grid, own, pieces, passing, result,
    load_sem, pair_send_sem, pair_recv_sem, edge_send_sem, edge_recv_sem,
    plane_send_sem, plane_recv_sem, passing_send_sem, passing_recv_sem, halo_send_sem, halo_recv_sem,
    piece_send_sem, piece_recv_sem,
):
    planes, rows, cols, depth_count, tile_count, groups = dims
    chips = depth_count // 2
    share = rows // depth_count
    block = 2 * share
    spacing = 3.0 / (planes * depth_count)
    group = share // groups
    me = lax.axis_index("depth")
    tile = lax.axis_index("tile")
    chip = me // 2
    core = me % 2
    stages = chips.bit_length() - 1
    assert chips == 1 << stages
    order = sorted(range(1, chips), key=lambda rel: (rel & -rel, -rel)) + [0]
    last = 2 * planes
    mine = pl.ds(1 + core * planes, planes)

    def relative(base, rel):
        for s in range(stages):
            if rel >> s & 1:
                base = base + (1 - 2 * (base // 2**s % 2)) * 2**s
        return base

    def remote(src, dst, send_sem, recv_sem, chip_to=chip, core_to=core, tile_to=tile):
        return pltpu.make_async_remote_copy(
            src_ref=src, dst_ref=dst, send_sem=send_sem, recv_sem=recv_sem,
            device_id=(chip_to * 2 + core_to, tile_to), device_id_type=pl.DeviceIdType.MESH,
        )

    has_front = chip > 0
    has_behind = chip < chips - 1
    has_low = tile > 0
    has_high = tile < tile_count - 1
    opposite = [relative(chip, 1 << s) for s in range(stages)]
    odd = chip % 2
    has_far = jnp.where(odd == 0, has_front, has_behind)
    far_chip = jnp.where(has_far, chip - 1 + 2 * odd, chip)

    barrier = pltpu.get_barrier_semaphore()

    def greet(cond, c, k, t):
        @pl.when(cond)
        def _():
            pl.semaphore_signal(barrier, inc=1, device_id=(c * 2 + k, t), device_id_type=pl.DeviceIdType.MESH)

    always = chip >= 0
    has_beside = jnp.where(core == 0, has_low, has_high)
    beside = tile - 1 + 2 * core
    far = core * (rows + 1)
    greet(has_beside, chip, 0, beside)
    greet(has_beside, chip, 1, beside)
    greet(has_far & (core == odd), far_chip, 1 - core, tile)
    greet(has_far, far_chip, core, tile)
    greet(always, opposite[0], 1 - core, tile)
    for c in opposite:
        greet(always, c, core, tile)
    greet(always, chip, 1 - core, tile)

    def count(cond):
        return cond.astype(jnp.int32)

    blank = jnp.zeros((SUB, LANE), jnp.float32)

    def load(p, count, k):
        return [
            pltpu.make_async_copy(
                field.at[pl.ds(p, count), :, pl.ds(j * LANE, LANE)],
                grid.at[pl.ds(1 + core * planes + p, count), pl.ds(1, rows), j, :],
                load_sem.at[k, j],
            )
            for j in range(cols // LANE)
        ]

    loads = [load(core * (planes - 1), 1, 0), load(1 - core, planes - 1, 1)]
    for copies in loads:
        for copy in copies:
            copy.start()

    @pl.when(jnp.logical_not(has_beside))
    def _():
        for p in range(last + 2):
            grid[p, far] = blank

    @pl.when(jnp.logical_not(has_behind))
    def _():
        grid[last + 1] = jnp.zeros(grid.shape[1:], jnp.float32)

    for copy in loads[0]:
        copy.wait()
    pl.semaphore_wait(barrier, 2 + stages + count(has_far) + count(has_far & (core == odd)) + count(has_low) + count(has_high))

    sent = []

    def begin(cond, copy):
        if cond is always:
            copy.start()
        else:
            pl.when(cond)(copy.start)
        sent.append((cond, copy))

    def drain():
        for cond, copy in sent:
            if cond is always:
                copy.wait_send()
            else:
                pl.when(cond)(copy.wait_send)
        sent.clear()

    def is_end(q, k):
        return jnp.where(k == 0, q == 0, q == chips - 1)

    evens = range(0, chips, 2)
    next_chip = [jnp.where(has_front, chip - 1, chip), jnp.where(has_behind, chip + 1, chip)]
    has_next = [has_front, has_behind]

    where = [relative(chip, rel) for rel in range(chips)]
    odds = [rel for rel in order if rel % 2]

    def windows(q, k):
        start = q * block + k * share
        end = is_end(q, k)
        skip = count(start == 0)
        return [
            (jnp.logical_not(end), pl.ds(start, share + 2), pl.ds(0, share + 2)),
            (end, pl.ds(start + skip, share + 1), pl.ds(skip, share + 1)),
        ]

    from_plane = 1 + core * (last - 1)
    to_plane = (1 - core) * (last + 1)
    meets = jnp.where(core == 0, next_chip[0], next_chip[1])
    has_meets = jnp.where(core == 0, has_front, has_behind)
    quarter = chip % 4
    def turns(rel, k):
        if stages < 2 or rel % 2 == 0:
            return chip < 0
        return always if rel % 4 in RELAY[0] and rel % 4 in RELAY[1] else (
            k == 0 if rel % 4 in RELAY[0] else k == 1 if rel % 4 in RELAY[1] else chip < 0
        )


    def planes_out(rel, k):
        q = where[rel]
        around = (quarter == 2 - core) & has_meets & turns(rel, core)
        due = has_meets & jnp.logical_not(around)
        if rel == 1 and k == 1:
            due = due & jnp.logical_not((odd == 1) & (core == 0))
        if rel == 0:
            due = due & (odd == 0) & (core == 1)
        slot = rel // 2
        for cond, at, local_at in windows(q, k):
            if rel % 2:
                begin(cond & around, remote(
                    grid.at[from_plane, at], passing.at[k, slot, local_at],
                    plane_send_sem.at[k, rel], passing_recv_sem.at[k, slot], opposite[1],
                ))
            begin(cond & due, remote(
                grid.at[from_plane, at], grid.at[to_plane, at],
                plane_send_sem.at[k, rel], plane_recv_sem.at[core, q], meets, k,
            ))

    def pass_on(rel):
        slot = rel // 2
        q = relative(opposite[1], rel)
        for k in range(2):
            for cond, at, local_at in windows(q, k):
                cond = cond & (quarter == 3 * core) & turns(rel, core)
                arriving = remote(
                    passing.at[k, slot, local_at], passing.at[k, slot, local_at],
                    passing_send_sem.at[k, slot], passing_recv_sem.at[k, slot], opposite[1],
                )
                pl.when(cond)(arriving.wait_recv)
                begin(cond, remote(
                    passing.at[k, slot, local_at], grid.at[to_plane, at],
                    passing_send_sem.at[k, slot], plane_recv_sem.at[core, q], opposite[0], k,
                ))

    def halo(kind):
        return remote(
            grid.at[1 + kind * (last - 1), far], grid.at[(1 - kind) * (last + 1), far],
            halo_send_sem.at[kind], halo_recv_sem.at[kind], next_chip[kind],
        )

    def from_next(kind, cond, rel):
        q = where[rel]
        for window, at, _ in windows(q, core):
            pl.when(cond & window)(remote(
                grid.at[(1 - kind) * (last + 1), at], grid.at[(1 - kind) * (last + 1), at],
                plane_send_sem.at[0, 0], plane_recv_sem.at[kind, q], core_to=1 - core,
            ).wait_recv)
        pl.when(cond & is_end(q, core) & has_beside)(halo(kind).wait_recv)

    planes_out(0, 1)
    for rel in odds:
        for k in range(2):
            planes_out(rel, k)

    for copies in loads[1:]:
        for copy in copies:
            copy.wait()

    theirs = pl.ds(1 + (1 - core) * planes, planes)

    def swap(step, rel, k, which):
        return [
            (cond, remote(
                grid.at[which, at], grid.at[which, at], pair_send_sem.at[step], pair_recv_sem.at[step], core_to=1 - core
            ))
            for cond, at, _ in windows(where[rel], k)
        ]

    def swapped(step, rel):
        for cond, copy in swap(step, rel, core, theirs):
            pl.when(cond)(copy.wait_recv)

    for step, rel in enumerate(order):
        for cond, copy in swap(step, rel, 1 - core, mine):
            begin(cond, copy)
        if step == 0:
            for k, (have, row, t) in enumerate(((has_high, rows, tile + 1), (has_low, 1, tile - 1))):
                begin(have, remote(
                    grid.at[mine, row], grid.at[mine, k * (rows + 1)], edge_send_sem.at[k], edge_recv_sem.at[core],
                    core_to=k, tile_to=t,
                ))

    def edges(cond):
        for k in range(2):
            which = pl.ds(1 + k * planes, planes)
            copy = remote(
                grid.at[which, far], grid.at[which, far], edge_send_sem.at[0], edge_recv_sem.at[k], core_to=1 - core
            )
            pl.when(cond & has_beside)(copy.wait_recv)

    lane = lax.broadcasted_iota(jnp.int32, (group, SUB, LANE), 2)
    sub = lax.broadcasted_iota(jnp.int32, (group, SUB, LANE), 1)
    left_edge = lane == 0
    right_edge = lane == LANE - 1
    left_end = left_edge & (sub == 0)
    right_end = right_edge & (sub == SUB - 1)
    scale = spacing * LOG2E

    def window(row):
        return pl.ds(row, group + 2)

    def plane_step(p, row, state):
        red, blue, green, through = state
        here = grid[p, window(row)]
        there = grid[p + 1, window(row)]
        total = here + there
        twice = total[1:-1]
        d_depth = there[1:-1] - here[1:-1]
        d_rows = total[2:] - total[:-2]
        from_left = pltpu.roll(twice, 1, 2)
        from_left = jnp.where(left_edge, pltpu.roll(from_left, 1, 1), from_left)
        from_left = jnp.where(left_end, 0.0, from_left)
        from_right = pltpu.roll(twice, LANE - 1, 2)
        from_right = jnp.where(right_edge, pltpu.roll(from_right, SUB - 1, 1), from_right)
        from_right = jnp.where(right_end, 0.0, from_right)
        d_cols = from_right - from_left
        facing = (0.25 * light_cols) * d_cols + (0.25 * light_rows) * d_rows + light_depth * d_depth
        length = (d_cols * d_cols + d_rows * d_rows) * 0.0625 + (d_depth * d_depth + 1.0)
        shading = 0.3 + 0.7 * jnp.abs(facing) * lax.rsqrt(length)
        optics = scale * floor_density
        for centre, width, bump in zip(centres, spreads, heights):
            root = math.sqrt(LOG2E) / width
            scaled = (0.5 * root) * twice - root * centre
            optics = optics + jnp.exp2(math.log2(bump * scale) - scaled * scaled)
        after = through * jnp.exp2(-optics)
        lit = (through - after) * shading
        middle = jnp.exp2((twice * (-0.25 * LOG2E)) * twice)
        balance = jnp.tanh(0.5 * twice)
        return (red + lit, blue + lit * balance, green + lit * middle, after)

    zero = jnp.zeros((group, SUB, LANE), jnp.float32)
    clear = (zero, zero, zero, zero + 1.0)
    def get(rel, at):
        return tuple(own[rel, c, at] for c in range(4))

    def put(rel, at, state):
        for c in range(4):
            own[rel, c, at] = state[c]

    def place(rel, i):
        turn = count(is_end(where[rel], core) & (core == 0))
        offset = (i + turn) % groups * group
        return pl.ds(offset, group), where[rel] * block + core * share + offset

    def near_state(row):
        state = clear
        for p in range(planes - 1):
            state = plane_step(1 + core * planes + p, row, state)
        return state

    def near_part(rel, low, high):
        def body(i, carry):
            at, row = place(rel, i)
            put(rel, at, near_state(row))
            return carry

        lax.fori_loop(low, high, body, 0)

    def compose(nearer, here, there):
        through = jnp.where(nearer, here[3], there[3])
        state = [
            jnp.where(nearer, here[c], there[c]) + through * jnp.where(nearer, there[c], here[c]) for c in range(3)
        ]
        return (*state, here[3] * there[3])

    def far_part(rel, low, high, both):
        def body(i, carry):
            at, row = place(rel, i)
            here = near_state(row) if both else get(rel, at)
            state = clear
            for p in range(planes):
                state = plane_step(planes - (planes - 1) * core + p, row, state)
            put(rel, at, compose(core == 0, here, state))
            return carry

        lax.fori_loop(low, high, body, 0)

    def in_front(rel, cond):
        start = where[rel] * block + core * share

        @pl.when(cond)
        def _():
            from_next(1, has_front, rel)

            def body(i, carry):
                at = pl.ds(i * group, group)
                red, blue, green, through = get(rel, at)
                first = plane_step(0, start + i * group, clear)
                put(rel, at, (
                    first[0] + first[3] * red, first[1] + first[3] * blue, first[2] + first[3] * green,
                    first[3] * through,
                ))
                return carry

            lax.fori_loop(0, groups, body, 0)

    def behind(rel, cond, low=0, high=groups):
        @pl.when(cond)
        def _():
            def body(i, carry):
                at, row = place(rel, i)
                put(rel, at, plane_step(last, row, get(rel, at)))
                return carry

            lax.fori_loop(low, high, body, 0)

    piece_copies = {}

    def forward(s, rel, i):
        j = rel >> (s + 1)
        slot = chips - (chips >> s) + j
        at, _ = place(rel, i)
        copy = remote(
            own.at[rel, :, at], pieces.at[slot, :, at], piece_send_sem.at[slot, i], piece_recv_sem.at[slot, i],
            opposite[s],
        )
        copy.start()
        piece_copies[s, j, i] = (copy, slot)

    for rel in order[:AHEAD]:
        near_part(rel, 0, groups - 1)
    def complete(step, rel, low, high):
        if low == high:
            return
        middle = min(high, groups - 1) if step < AHEAD else low
        if low < middle:
            far_part(rel, low, middle, False)
        if middle < high:
            far_part(rel, middle, high, True)
        if rel % 2:
            if rel == 1 and high == groups:
                in_front(rel, (odd == 1) & (core == 1))
            behind(rel, jnp.logical_not(has_behind), low, high)
            for i in range(low, high):
                forward(0, rel, i)

    swapped(0, order[0])
    for rel in odds:
        pass_on(rel)
    far_part(order[0], 0, groups - 1, False)
    edges(always)
    for kind in range(2):
        begin(has_next[kind] & has_beside & ((chip + core) % 2 == 1), halo(kind))
    far_part(order[0], groups - 1, groups, True)
    behind(order[0], jnp.logical_not(has_behind))
    for i in range(groups):
        forward(0, order[0], i)
    for step, rel in enumerate(order[1:], 1):
        swapped(step, rel)
        complete(step, rel, 0, groups)

    def interfaces(rel):
        in_front(rel, has_front)
        if rel == 0:
            from_next(0, has_behind & ((odd == 1) | (core == 0)), rel)
            behind(rel, (odd == 1) | (core == 0))
        else:
            from_next(0, has_behind, rel)
            behind(rel, always)

    def received(s, j, i, state):
        rel = j << (s + 1)
        at, _ = place(rel, i)
        copy, slot = piece_copies[s, j, i]
        copy.wait_recv()
        return compose(chip // 2**s % 2 == 0, state, [pieces[slot, c, at] for c in range(4)])

    for s in range(stages):
        for j in reversed(range(1, chips >> (s + 1))):
            rel = j << (s + 1)
            if s == 0:
                interfaces(rel)
            for i in range(groups):
                at, _ = place(rel, i)
                put(rel, at, received(s, j, i, get(rel, at)))
                if j % 2:
                    forward(s + 1, rel, i)
    interfaces(0)
    drain()
    for i in range(groups):
        at, _ = place(0, i)
        state = get(0, at)
        for s in range(stages):
            state = received(s, 0, i, state)
        image = (0.5 * (state[0] + state[1]), state[2], 0.5 * (state[0] - state[1]), 1.0 - state[3])
        for c in range(4):
            result[at, c * SUB : (c + 1) * SUB, :] = image[c]
        for b in range(cols // LANE):
            out[at, :, b * LANE : (b + 1) * LANE] = result[at, pl.ds(b, 4, stride=SUB), :]

    for copy, _ in piece_copies.values():
        copy.wait_send()


def local(field):
    planes, rows, cols = field.shape
    depth_count = lax.axis_size("depth")
    chips = depth_count // 2
    share = rows // depth_count
    f32 = jnp.float32
    groups = min(share // g for g in range(1, 5) if share % g == 0)
    dims = (planes, rows, cols, depth_count, lax.axis_size("tile"), groups)
    dma = pltpu.SemaphoreType.DMA
    image = pl.pallas_call(
        functools.partial(kernel, dims),
        out_shape=jax.ShapeDtypeStruct((share, 4, cols), f32),
        in_specs=[pl.BlockSpec(memory_space=pltpu.HBM)],
        out_specs=pl.BlockSpec(memory_space=pltpu.VMEM),
        scratch_shapes=[
            pltpu.VMEM((2 * planes + 2, rows + 2, SUB, LANE), f32),
            pltpu.VMEM((chips, 4, share, SUB, LANE), f32),
            pltpu.VMEM((chips - 1, 4, share, SUB, LANE), f32),
            pltpu.VMEM((2, chips // 2, share + 2, SUB, LANE), f32),
            pltpu.VMEM((share, 4 * SUB, LANE), f32),
            dma((2, cols // LANE)),
            dma((chips,)),
            dma((chips,)),
            dma((2,)),
            dma((2,)),
            dma((2, chips)),
            dma((2, chips)),
            dma((2, chips // 2)),
            dma((2, chips // 2)),
            dma((2,)),
            dma((2,)),
            dma((chips - 1, groups)),
            dma((chips - 1, groups)),
        ],
        compiler_params=pltpu.CompilerParams(
            collective_id=0, has_side_effects=True, vmem_limit_bytes=55_000_000
        ),
    )(field)
    return jnp.transpose(image, (1, 0, 2))


def solution(mesh):
    return jax.shard_map(
        local,
        mesh=mesh,
        in_specs=(P("depth", "tile", None),),
        out_specs=P(None, ("tile", "depth"), None),
        check_vma=False,
    )
```

```python
import functools
import math

import jax
import jax.numpy as jnp
from jax import lax
from jax.experimental import pallas as pl
from jax.experimental.pallas import tpu as pltpu
from jax.sharding import PartitionSpec as P

centres = (-1.2, 0.3, 1.5)
spreads = (0.25, 0.35, 0.3)
heights = (2.0, 1.0, 3.0)
floor_density = 0.05
light_cols = 0.48
light_rows = 0.6
light_depth = 0.64

LOG2E = math.log2(math.e)
SUB, LANE = 8, 128
RELAY = ((1,), (3,))
AHEAD = 4


def kernel(
    dims, field, out, grid, own, pieces, passing, result,
    load_sem, pair_send_sem, pair_recv_sem, edge_send_sem, edge_recv_sem,
    plane_send_sem, plane_recv_sem, passing_send_sem, passing_recv_sem, halo_send_sem, halo_recv_sem,
    piece_send_sem, piece_recv_sem,
):
    planes, rows, cols, depth_count, tile_count, groups = dims
    chips = depth_count // 2
    share = rows // depth_count
    block = 2 * share
    spacing = 3.0 / (planes * depth_count)
    group = share // groups
    me = lax.axis_index("depth")
    tile = lax.axis_index("tile")
    chip = me // 2
    core = me % 2
    stages = chips.bit_length() - 1
    assert chips == 1 << stages
    order = sorted(range(1, chips), key=lambda rel: (rel & -rel, -rel)) + [0]
    last = 2 * planes
    mine = pl.ds(1 + core * planes, planes)

    def relative(base, rel):
        for s in range(stages):
            if rel >> s & 1:
                base = base + (1 - 2 * (base // 2**s % 2)) * 2**s
        return base

    def remote(src, dst, send_sem, recv_sem, chip_to=chip, core_to=core, tile_to=tile):
        return pltpu.make_async_remote_copy(
            src_ref=src, dst_ref=dst, send_sem=send_sem, recv_sem=recv_sem,
            device_id=(chip_to * 2 + core_to, tile_to), device_id_type=pl.DeviceIdType.MESH,
        )

    has_front = chip > 0
    has_behind = chip < chips - 1
    has_low = tile > 0
    has_high = tile < tile_count - 1
    opposite = [relative(chip, 1 << s) for s in range(stages)]
    odd = chip % 2
    has_far = jnp.where(odd == 0, has_front, has_behind)
    far_chip = jnp.where(has_far, chip - 1 + 2 * odd, chip)

    barrier = pltpu.get_barrier_semaphore()

    def greet(cond, c, k, t):
        @pl.when(cond)
        def _():
            pl.semaphore_signal(barrier, inc=1, device_id=(c * 2 + k, t), device_id_type=pl.DeviceIdType.MESH)

    always = chip >= 0
    has_beside = jnp.where(core == 0, has_low, has_high)
    beside = tile - 1 + 2 * core
    far = core * (rows + 1)
    greet(has_beside, chip, 0, beside)
    greet(has_beside, chip, 1, beside)
    greet(has_far & (core == odd), far_chip, 1 - core, tile)
    greet(has_far, far_chip, core, tile)
    greet(always, opposite[0], 1 - core, tile)
    for c in opposite:
        greet(always, c, core, tile)
    greet(always, chip, 1 - core, tile)

    def count(cond):
        return cond.astype(jnp.int32)

    blank = jnp.zeros((SUB, LANE), jnp.float32)

    def load(p, count, k):
        return [
            pltpu.make_async_copy(
                field.at[pl.ds(p, count), :, pl.ds(j * LANE, LANE)],
                grid.at[pl.ds(1 + core * planes + p, count), pl.ds(1, rows), j, :],
                load_sem.at[k, j],
            )
            for j in range(cols // LANE)
        ]

    loads = [load(core * (planes - 1), 1, 0), load(1 - core, planes - 1, 1)]
    for copies in loads:
        for copy in copies:
            copy.start()

    @pl.when(jnp.logical_not(has_beside))
    def _():
        for p in range(last + 2):
            grid[p, far] = blank

    @pl.when(jnp.logical_not(has_behind))
    def _():
        grid[last + 1] = jnp.zeros(grid.shape[1:], jnp.float32)

    for copy in loads[0]:
        copy.wait()
    pl.semaphore_wait(barrier, 2 + stages + count(has_far) + count(has_far & (core == odd)) + count(has_low) + count(has_high))

    sent = []

    def begin(cond, copy):
        if cond is always:
            copy.start()
        else:
            pl.when(cond)(copy.start)
        sent.append((cond, copy))

    def drain():
        for cond, copy in sent:
            if cond is always:
                copy.wait_send()
            else:
                pl.when(cond)(copy.wait_send)
        sent.clear()

    def is_end(q, k):
        return jnp.where(k == 0, q == 0, q == chips - 1)

    evens = range(0, chips, 2)
    next_chip = [jnp.where(has_front, chip - 1, chip), jnp.where(has_behind, chip + 1, chip)]
    has_next = [has_front, has_behind]

    where = [relative(chip, rel) for rel in range(chips)]
    odds = [rel for rel in order if rel % 2]

    def windows(q, k):
        start = q * block + k * share
        end = is_end(q, k)
        skip = count(start == 0)
        return [
            (jnp.logical_not(end), pl.ds(start, share + 2), pl.ds(0, share + 2)),
            (end, pl.ds(start + skip, share + 1), pl.ds(skip, share + 1)),
        ]

    from_plane = 1 + core * (last - 1)
    to_plane = (1 - core) * (last + 1)
    meets = jnp.where(core == 0, next_chip[0], next_chip[1])
    has_meets = jnp.where(core == 0, has_front, has_behind)
    quarter = chip % 4
    def turns(rel, k):
        if stages < 2 or rel % 2 == 0:
            return chip < 0
        return always if rel % 4 in RELAY[0] and rel % 4 in RELAY[1] else (
            k == 0 if rel % 4 in RELAY[0] else k == 1 if rel % 4 in RELAY[1] else chip < 0
        )


    def planes_out(rel, k):
        q = where[rel]
        around = (quarter == 2 - core) & has_meets & turns(rel, core)
        due = has_meets & jnp.logical_not(around)
        if rel == 1 and k == 1:
            due = due & jnp.logical_not((odd == 1) & (core == 0))
        if rel == 0:
            due = due & (odd == 0) & (core == 1)
        slot = rel // 2
        for cond, at, local_at in windows(q, k):
            if rel % 2:
                begin(cond & around, remote(
                    grid.at[from_plane, at], passing.at[k, slot, local_at],
                    plane_send_sem.at[k, rel], passing_recv_sem.at[k, slot], opposite[1],
                ))
            begin(cond & due, remote(
                grid.at[from_plane, at], grid.at[to_plane, at],
                plane_send_sem.at[k, rel], plane_recv_sem.at[core, q], meets, k,
            ))

    def pass_on(rel):
        slot = rel // 2
        q = relative(opposite[1], rel)
        for k in range(2):
            for cond, at, local_at in windows(q, k):
                cond = cond & (quarter == 3 * core) & turns(rel, core)
                arriving = remote(
                    passing.at[k, slot, local_at], passing.at[k, slot, local_at],
                    passing_send_sem.at[k, slot], passing_recv_sem.at[k, slot], opposite[1],
                )
                pl.when(cond)(arriving.wait_recv)
                begin(cond, remote(
                    passing.at[k, slot, local_at], grid.at[to_plane, at],
                    passing_send_sem.at[k, slot], plane_recv_sem.at[core, q], opposite[0], k,
                ))

    def halo(kind):
        return remote(
            grid.at[1 + kind * (last - 1), far], grid.at[(1 - kind) * (last + 1), far],
            halo_send_sem.at[kind], halo_recv_sem.at[kind], next_chip[kind],
        )

    def from_next(kind, cond, rel):
        q = where[rel]
        for window, at, _ in windows(q, core):
            pl.when(cond & window)(remote(
                grid.at[(1 - kind) * (last + 1), at], grid.at[(1 - kind) * (last + 1), at],
                plane_send_sem.at[0, 0], plane_recv_sem.at[kind, q], core_to=1 - core,
            ).wait_recv)
        pl.when(cond & is_end(q, core) & has_beside)(halo(kind).wait_recv)

    planes_out(0, 1)
    for rel in odds:
        for k in range(2):
            planes_out(rel, k)

    for copies in loads[1:]:
        for copy in copies:
            copy.wait()

    theirs = pl.ds(1 + (1 - core) * planes, planes)

    def swap(step, rel, k, which):
        return [
            (cond, remote(
                grid.at[which, at], grid.at[which, at], pair_send_sem.at[step], pair_recv_sem.at[step], core_to=1 - core
            ))
            for cond, at, _ in windows(where[rel], k)
        ]

    def swapped(step, rel):
        for cond, copy in swap(step, rel, core, theirs):
            pl.when(cond)(copy.wait_recv)

    for step, rel in enumerate(order):
        for cond, copy in swap(step, rel, 1 - core, mine):
            begin(cond, copy)
        if step == 0:
            for k, (have, row, t) in enumerate(((has_high, rows, tile + 1), (has_low, 1, tile - 1))):
                begin(have, remote(
                    grid.at[mine, row], grid.at[mine, k * (rows + 1)], edge_send_sem.at[k], edge_recv_sem.at[core],
                    core_to=k, tile_to=t,
                ))

    def edges(cond):
        for k in range(2):
            which = pl.ds(1 + k * planes, planes)
            copy = remote(
                grid.at[which, far], grid.at[which, far], edge_send_sem.at[0], edge_recv_sem.at[k], core_to=1 - core
            )
            pl.when(cond & has_beside)(copy.wait_recv)

    lane = lax.broadcasted_iota(jnp.int32, (group, SUB, LANE), 2)
    sub = lax.broadcasted_iota(jnp.int32, (group, SUB, LANE), 1)
    left_edge = lane == 0
    right_edge = lane == LANE - 1
    left_end = left_edge & (sub == 0)
    right_end = right_edge & (sub == SUB - 1)
    scale = spacing * LOG2E

    def window(row):
        return pl.ds(row, group + 2)

    def plane_step(p, row, state):
        red, blue, green, through = state
        here = grid[p, window(row)]
        there = grid[p + 1, window(row)]
        total = here + there
        twice = total[1:-1]
        d_depth = there[1:-1] - here[1:-1]
        d_rows = total[2:] - total[:-2]
        from_left = pltpu.roll(twice, 1, 2)
        from_left = jnp.where(left_edge, pltpu.roll(from_left, 1, 1), from_left)
        from_left = jnp.where(left_end, 0.0, from_left)
        from_right = pltpu.roll(twice, LANE - 1, 2)
        from_right = jnp.where(right_edge, pltpu.roll(from_right, SUB - 1, 1), from_right)
        from_right = jnp.where(right_end, 0.0, from_right)
        d_cols = from_right - from_left
        facing = (0.25 * light_cols) * d_cols + (0.25 * light_rows) * d_rows + light_depth * d_depth
        length = (d_cols * d_cols + d_rows * d_rows) * 0.0625 + (d_depth * d_depth + 1.0)
        shading = 0.3 + 0.7 * jnp.abs(facing) * lax.rsqrt(length)
        optics = scale * floor_density
        for centre, width, bump in zip(centres, spreads, heights):
            root = math.sqrt(LOG2E) / width
            scaled = (0.5 * root) * twice - root * centre
            optics = optics + jnp.exp2(math.log2(bump * scale) - scaled * scaled)
        after = through * jnp.exp2(-optics)
        lit = (through - after) * shading
        middle = jnp.exp2((twice * (-0.25 * LOG2E)) * twice)
        balance = jnp.tanh(0.5 * twice)
        return (red + lit, blue + lit * balance, green + lit * middle, after)

    zero = jnp.zeros((group, SUB, LANE), jnp.float32)
    clear = (zero, zero, zero, zero + 1.0)
    def get(rel, at):
        return tuple(own[rel, c, at] for c in range(4))

    def put(rel, at, state):
        for c in range(4):
            own[rel, c, at] = state[c]

    def place(rel, i):
        turn = count(is_end(where[rel], core) & (core == 0))
        offset = (i + turn) % groups * group
        return pl.ds(offset, group), where[rel] * block + core * share + offset

    def near_state(row):
        state = clear
        for p in range(planes - 1):
            state = plane_step(1 + core * planes + p, row, state)
        return state

    def near_part(rel, low, high):
        def body(i, carry):
            at, row = place(rel, i)
            put(rel, at, near_state(row))
            return carry

        lax.fori_loop(low, high, body, 0)

    def compose(nearer, here, there):
        through = jnp.where(nearer, here[3], there[3])
        state = [
            jnp.where(nearer, here[c], there[c]) + through * jnp.where(nearer, there[c], here[c]) for c in range(3)
        ]
        return (*state, here[3] * there[3])

    def far_part(rel, low, high, both):
        def body(i, carry):
            at, row = place(rel, i)
            here = near_state(row) if both else get(rel, at)
            state = clear
            for p in range(planes):
                state = plane_step(planes - (planes - 1) * core + p, row, state)
            put(rel, at, compose(core == 0, here, state))
            return carry

        lax.fori_loop(low, high, body, 0)

    def in_front(rel, cond):
        start = where[rel] * block + core * share

        @pl.when(cond)
        def _():
            from_next(1, has_front, rel)

            def body(i, carry):
                at = pl.ds(i * group, group)
                red, blue, green, through = get(rel, at)
                first = plane_step(0, start + i * group, clear)
                put(rel, at, (
                    first[0] + first[3] * red, first[1] + first[3] * blue, first[2] + first[3] * green,
                    first[3] * through,
                ))
                return carry

            lax.fori_loop(0, groups, body, 0)

    def behind(rel, cond, low=0, high=groups):
        @pl.when(cond)
        def _():
            def body(i, carry):
                at, row = place(rel, i)
                put(rel, at, plane_step(last, row, get(rel, at)))
                return carry

            lax.fori_loop(low, high, body, 0)

    piece_copies = {}

    def forward(s, rel, i):
        j = rel >> (s + 1)
        slot = chips - (chips >> s) + j
        at, _ = place(rel, i)
        copy = remote(
            own.at[rel, :, at], pieces.at[slot, :, at], piece_send_sem.at[slot, i], piece_recv_sem.at[slot, i],
            opposite[s],
        )
        copy.start()
        piece_copies[s, j, i] = (copy, slot)

    for rel in order[:AHEAD]:
        near_part(rel, 0, groups - 1)
    def complete(step, rel, low, high):
        if low == high:
            return
        middle = min(high, groups - 1) if step < AHEAD else low
        if low < middle:
            far_part(rel, low, middle, False)
        if middle < high:
            far_part(rel, middle, high, True)
        if rel % 2:
            if rel == 1 and high == groups:
                in_front(rel, (odd == 1) & (core == 1))
            behind(rel, jnp.logical_not(has_behind), low, high)
            for i in range(low, high):
                forward(0, rel, i)

    swapped(0, order[0])
    for rel in odds:
        pass_on(rel)
    far_part(order[0], 0, groups - 1, False)
    edges(always)
    for kind in range(2):
        begin(has_next[kind] & has_beside & ((chip + core) % 2 == 1), halo(kind))
    behind(order[0], jnp.logical_not(has_behind), 0, groups - 1)
    for i in range(groups - 1):
        forward(0, order[0], i)
    complete(0, order[0], groups - 1, groups)
    for step, rel in enumerate(order[1:], 1):
        swapped(step, rel)
        complete(step, rel, 0, groups)

    def interfaces(rel):
        in_front(rel, has_front)
        if rel == 0:
            from_next(0, has_behind & ((odd == 1) | (core == 0)), rel)
            behind(rel, (odd == 1) | (core == 0))
        else:
            from_next(0, has_behind, rel)
            behind(rel, always)

    def received(s, j, i, state):
        rel = j << (s + 1)
        at, _ = place(rel, i)
        copy, slot = piece_copies[s, j, i]
        copy.wait_recv()
        return compose(chip // 2**s % 2 == 0, state, [pieces[slot, c, at] for c in range(4)])

    for s in range(stages):
        for j in reversed(range(1, chips >> (s + 1))):
            rel = j << (s + 1)
            if s == 0:
                interfaces(rel)
            for i in range(groups):
                at, _ = place(rel, i)
                put(rel, at, received(s, j, i, get(rel, at)))
                if j % 2:
                    forward(s + 1, rel, i)
    interfaces(0)
    drain()
    for i in range(groups):
        at, _ = place(0, i)
        state = get(0, at)
        for s in range(stages):
            state = received(s, 0, i, state)
        image = (0.5 * (state[0] + state[1]), state[2], 0.5 * (state[0] - state[1]), 1.0 - state[3])
        for c in range(4):
            result[at, c * SUB : (c + 1) * SUB, :] = image[c]
        for b in range(cols // LANE):
            out[at, :, b * LANE : (b + 1) * LANE] = result[at, pl.ds(b, 4, stride=SUB), :]

    for copy, _ in piece_copies.values():
        copy.wait_send()


def local(field):
    planes, rows, cols = field.shape
    depth_count = lax.axis_size("depth")
    chips = depth_count // 2
    share = rows // depth_count
    f32 = jnp.float32
    groups = min(share // g for g in range(1, 5) if share % g == 0)
    dims = (planes, rows, cols, depth_count, lax.axis_size("tile"), groups)
    dma = pltpu.SemaphoreType.DMA
    image = pl.pallas_call(
        functools.partial(kernel, dims),
        out_shape=jax.ShapeDtypeStruct((share, 4, cols), f32),
        in_specs=[pl.BlockSpec(memory_space=pltpu.HBM)],
        out_specs=pl.BlockSpec(memory_space=pltpu.VMEM),
        scratch_shapes=[
            pltpu.VMEM((2 * planes + 2, rows + 2, SUB, LANE), f32),
            pltpu.VMEM((chips, 4, share, SUB, LANE), f32),
            pltpu.VMEM((chips - 1, 4, share, SUB, LANE), f32),
            pltpu.VMEM((2, chips // 2, share + 2, SUB, LANE), f32),
            pltpu.VMEM((share, 4 * SUB, LANE), f32),
            dma((2, cols // LANE)),
            dma((chips,)),
            dma((chips,)),
            dma((2,)),
            dma((2,)),
            dma((2, chips)),
            dma((2, chips)),
            dma((2, chips // 2)),
            dma((2, chips // 2)),
            dma((2,)),
            dma((2,)),
            dma((chips - 1, groups)),
            dma((chips - 1, groups)),
        ],
        compiler_params=pltpu.CompilerParams(
            collective_id=0, has_side_effects=True, vmem_limit_bytes=55_000_000
        ),
    )(field)
    return jnp.transpose(image, (1, 0, 2))


def solution(mesh):
    return jax.shard_map(
        local,
        mesh=mesh,
        in_specs=(P("depth", "tile", None),),
        out_specs=P(None, ("tile", "depth"), None),
        check_vma=False,
    )
```

```python
import functools
import math

import jax
import jax.numpy as jnp
from jax import lax
from jax.experimental import pallas as pl
from jax.experimental.pallas import tpu as pltpu
from jax.sharding import PartitionSpec as P

centres = (-1.2, 0.3, 1.5)
spreads = (0.25, 0.35, 0.3)
heights = (2.0, 1.0, 3.0)
floor_density = 0.05
light_cols = 0.48
light_rows = 0.6
light_depth = 0.64

LOG2E = math.log2(math.e)
SUB, LANE = 8, 128
RELAY = ((1,), (3,))
AHEAD = 4


def kernel(
    dims, field, out, grid, own, pieces, passing, result,
    load_sem, pair_send_sem, pair_recv_sem, edge_send_sem, edge_recv_sem,
    plane_send_sem, plane_recv_sem, passing_send_sem, passing_recv_sem, halo_send_sem, halo_recv_sem,
    piece_send_sem, piece_recv_sem,
):
    planes, rows, cols, depth_count, tile_count, groups = dims
    chips = depth_count // 2
    share = rows // depth_count
    block = 2 * share
    spacing = 3.0 / (planes * depth_count)
    group = share // groups
    me = lax.axis_index("depth")
    tile = lax.axis_index("tile")
    chip = me // 2
    core = me % 2
    stages = chips.bit_length() - 1
    assert chips == 1 << stages
    order = sorted(range(1, chips), key=lambda rel: (rel & -rel, -rel)) + [0]
    last = 2 * planes
    mine = pl.ds(1 + core * planes, planes)

    def relative(base, rel):
        for s in range(stages):
            if rel >> s & 1:
                base = base + (1 - 2 * (base // 2**s % 2)) * 2**s
        return base

    def remote(src, dst, send_sem, recv_sem, chip_to=chip, core_to=core, tile_to=tile):
        return pltpu.make_async_remote_copy(
            src_ref=src, dst_ref=dst, send_sem=send_sem, recv_sem=recv_sem,
            device_id=(chip_to * 2 + core_to, tile_to), device_id_type=pl.DeviceIdType.MESH,
        )

    has_front = chip > 0
    has_behind = chip < chips - 1
    has_low = tile > 0
    has_high = tile < tile_count - 1
    opposite = [relative(chip, 1 << s) for s in range(stages)]
    odd = chip % 2
    has_far = jnp.where(odd == 0, has_front, has_behind)
    far_chip = jnp.where(has_far, chip - 1 + 2 * odd, chip)

    barrier = pltpu.get_barrier_semaphore()

    def greet(cond, c, k, t):
        @pl.when(cond)
        def _():
            pl.semaphore_signal(barrier, inc=1, device_id=(c * 2 + k, t), device_id_type=pl.DeviceIdType.MESH)

    always = chip >= 0
    has_beside = jnp.where(core == 0, has_low, has_high)
    beside = tile - 1 + 2 * core
    far = core * (rows + 1)
    greet(has_beside, chip, 0, beside)
    greet(has_beside, chip, 1, beside)
    greet(has_far & (core == odd), far_chip, 1 - core, tile)
    greet(has_far, far_chip, core, tile)
    greet(always, opposite[0], 1 - core, tile)
    for c in opposite:
        greet(always, c, core, tile)
    greet(always, chip, 1 - core, tile)

    def count(cond):
        return cond.astype(jnp.int32)

    blank = jnp.zeros((SUB, LANE), jnp.float32)

    def load(p, count, k):
        return [
            pltpu.make_async_copy(
                field.at[pl.ds(p, count), :, pl.ds(j * LANE, LANE)],
                grid.at[pl.ds(1 + core * planes + p, count), pl.ds(1, rows), j, :],
                load_sem.at[k, j],
            )
            for j in range(cols // LANE)
        ]

    loads = [load(0, planes, 0)]
    for copies in loads:
        for copy in copies:
            copy.start()

    @pl.when(jnp.logical_not(has_beside))
    def _():
        for p in range(last + 2):
            grid[p, far] = blank

    @pl.when(jnp.logical_not(has_behind))
    def _():
        grid[last + 1] = jnp.zeros(grid.shape[1:], jnp.float32)

    for copy in loads[0]:
        copy.wait()
    pl.semaphore_wait(barrier, 2 + stages + count(has_far) + count(has_far & (core == odd)) + count(has_low) + count(has_high))

    sent = []

    def begin(cond, copy):
        if cond is always:
            copy.start()
        else:
            pl.when(cond)(copy.start)
        sent.append((cond, copy))

    def drain():
        for cond, copy in sent:
            if cond is always:
                copy.wait_send()
            else:
                pl.when(cond)(copy.wait_send)
        sent.clear()

    def is_end(q, k):
        return jnp.where(k == 0, q == 0, q == chips - 1)

    evens = range(0, chips, 2)
    next_chip = [jnp.where(has_front, chip - 1, chip), jnp.where(has_behind, chip + 1, chip)]
    has_next = [has_front, has_behind]

    where = [relative(chip, rel) for rel in range(chips)]
    odds = [rel for rel in order if rel % 2]

    def windows(q, k):
        start = q * block + k * share
        end = is_end(q, k)
        skip = count(start == 0)
        return [
            (jnp.logical_not(end), pl.ds(start, share + 2), pl.ds(0, share + 2)),
            (end, pl.ds(start + skip, share + 1), pl.ds(skip, share + 1)),
        ]

    from_plane = 1 + core * (last - 1)
    to_plane = (1 - core) * (last + 1)
    meets = jnp.where(core == 0, next_chip[0], next_chip[1])
    has_meets = jnp.where(core == 0, has_front, has_behind)
    quarter = chip % 4
    def turns(rel, k):
        if stages < 2 or rel % 2 == 0:
            return chip < 0
        return always if rel % 4 in RELAY[0] and rel % 4 in RELAY[1] else (
            k == 0 if rel % 4 in RELAY[0] else k == 1 if rel % 4 in RELAY[1] else chip < 0
        )


    def planes_out(rel, k):
        q = where[rel]
        around = (quarter == 2 - core) & has_meets & turns(rel, core)
        due = has_meets & jnp.logical_not(around)
        if rel == 1 and k == 1:
            due = due & jnp.logical_not((odd == 1) & (core == 0))
        if rel == 0:
            due = due & (odd == 0) & (core == 1)
        slot = rel // 2
        for cond, at, local_at in windows(q, k):
            if rel % 2:
                begin(cond & around, remote(
                    grid.at[from_plane, at], passing.at[k, slot, local_at],
                    plane_send_sem.at[k, rel], passing_recv_sem.at[k, slot], opposite[1],
                ))
            begin(cond & due, remote(
                grid.at[from_plane, at], grid.at[to_plane, at],
                plane_send_sem.at[k, rel], plane_recv_sem.at[core, q], meets, k,
            ))

    def pass_on(rel):
        slot = rel // 2
        q = relative(opposite[1], rel)
        for k in range(2):
            for cond, at, local_at in windows(q, k):
                cond = cond & (quarter == 3 * core) & turns(rel, core)
                arriving = remote(
                    passing.at[k, slot, local_at], passing.at[k, slot, local_at],
                    passing_send_sem.at[k, slot], passing_recv_sem.at[k, slot], opposite[1],
                )
                pl.when(cond)(arriving.wait_recv)
                begin(cond, remote(
                    passing.at[k, slot, local_at], grid.at[to_plane, at],
                    passing_send_sem.at[k, slot], plane_recv_sem.at[core, q], opposite[0], k,
                ))

    def halo(kind):
        return remote(
            grid.at[1 + kind * (last - 1), far], grid.at[(1 - kind) * (last + 1), far],
            halo_send_sem.at[kind], halo_recv_sem.at[kind], next_chip[kind],
        )

    def from_next(kind, cond, rel):
        q = where[rel]
        for window, at, _ in windows(q, core):
            pl.when(cond & window)(remote(
                grid.at[(1 - kind) * (last + 1), at], grid.at[(1 - kind) * (last + 1), at],
                plane_send_sem.at[0, 0], plane_recv_sem.at[kind, q], core_to=1 - core,
            ).wait_recv)
        pl.when(cond & is_end(q, core) & has_beside)(halo(kind).wait_recv)

    planes_out(0, 1)
    for rel in odds:
        for k in range(2):
            planes_out(rel, k)

    for copies in loads[1:]:
        for copy in copies:
            copy.wait()

    theirs = pl.ds(1 + (1 - core) * planes, planes)

    def swap(step, rel, k, which):
        return [
            (cond, remote(
                grid.at[which, at], grid.at[which, at], pair_send_sem.at[step], pair_recv_sem.at[step], core_to=1 - core
            ))
            for cond, at, _ in windows(where[rel], k)
        ]

    def swapped(step, rel):
        for cond, copy in swap(step, rel, core, theirs):
            pl.when(cond)(copy.wait_recv)

    for step, rel in enumerate(order):
        for cond, copy in swap(step, rel, 1 - core, mine):
            begin(cond, copy)
        if step == 0:
            for k, (have, row, t) in enumerate(((has_high, rows, tile + 1), (has_low, 1, tile - 1))):
                begin(have, remote(
                    grid.at[mine, row], grid.at[mine, k * (rows + 1)], edge_send_sem.at[k], edge_recv_sem.at[core],
                    core_to=k, tile_to=t,
                ))

    def edges(cond):
        for k in range(2):
            which = pl.ds(1 + k * planes, planes)
            copy = remote(
                grid.at[which, far], grid.at[which, far], edge_send_sem.at[0], edge_recv_sem.at[k], core_to=1 - core
            )
            pl.when(cond & has_beside)(copy.wait_recv)

    lane = lax.broadcasted_iota(jnp.int32, (group, SUB, LANE), 2)
    sub = lax.broadcasted_iota(jnp.int32, (group, SUB, LANE), 1)
    left_edge = lane == 0
    right_edge = lane == LANE - 1
    left_end = left_edge & (sub == 0)
    right_end = right_edge & (sub == SUB - 1)
    scale = spacing * LOG2E

    def window(row):
        return pl.ds(row, group + 2)

    def plane_step(p, row, state):
        red, blue, green, through = state
        here = grid[p, window(row)]
        there = grid[p + 1, window(row)]
        total = here + there
        twice = total[1:-1]
        d_depth = there[1:-1] - here[1:-1]
        d_rows = total[2:] - total[:-2]
        from_left = pltpu.roll(twice, 1, 2)
        from_left = jnp.where(left_edge, pltpu.roll(from_left, 1, 1), from_left)
        from_left = jnp.where(left_end, 0.0, from_left)
        from_right = pltpu.roll(twice, LANE - 1, 2)
        from_right = jnp.where(right_edge, pltpu.roll(from_right, SUB - 1, 1), from_right)
        from_right = jnp.where(right_end, 0.0, from_right)
        d_cols = from_right - from_left
        facing = (0.25 * light_cols) * d_cols + (0.25 * light_rows) * d_rows + light_depth * d_depth
        length = (d_cols * d_cols + d_rows * d_rows) * 0.0625 + (d_depth * d_depth + 1.0)
        shading = 0.3 + 0.7 * jnp.abs(facing) * lax.rsqrt(length)
        optics = scale * floor_density
        for centre, width, bump in zip(centres, spreads, heights):
            root = math.sqrt(LOG2E) / width
            scaled = (0.5 * root) * twice - root * centre
            optics = optics + jnp.exp2(math.log2(bump * scale) - scaled * scaled)
        after = through * jnp.exp2(-optics)
        lit = (through - after) * shading
        middle = jnp.exp2((twice * (-0.25 * LOG2E)) * twice)
        balance = jnp.tanh(0.5 * twice)
        return (red + lit, blue + lit * balance, green + lit * middle, after)

    zero = jnp.zeros((group, SUB, LANE), jnp.float32)
    clear = (zero, zero, zero, zero + 1.0)
    def get(rel, at):
        return tuple(own[rel, c, at] for c in range(4))

    def put(rel, at, state):
        for c in range(4):
            own[rel, c, at] = state[c]

    def place(rel, i):
        turn = count(is_end(where[rel], core) & (core == 0))
        offset = (i + turn) % groups * group
        return pl.ds(offset, group), where[rel] * block + core * share + offset

    def near_state(row):
        state = clear
        for p in range(planes - 1):
            state = plane_step(1 + core * planes + p, row, state)
        return state

    def near_part(rel, low, high):
        def body(i, carry):
            at, row = place(rel, i)
            put(rel, at, near_state(row))
            return carry

        lax.fori_loop(low, high, body, 0)

    def compose(nearer, here, there):
        through = jnp.where(nearer, here[3], there[3])
        state = [
            jnp.where(nearer, here[c], there[c]) + through * jnp.where(nearer, there[c], here[c]) for c in range(3)
        ]
        return (*state, here[3] * there[3])

    def far_part(rel, low, high, both):
        def body(i, carry):
            at, row = place(rel, i)
            here = near_state(row) if both else get(rel, at)
            state = clear
            for p in range(planes):
                state = plane_step(planes - (planes - 1) * core + p, row, state)
            put(rel, at, compose(core == 0, here, state))
            return carry

        lax.fori_loop(low, high, body, 0)

    def in_front(rel, cond):
        start = where[rel] * block + core * share

        @pl.when(cond)
        def _():
            from_next(1, has_front, rel)

            def body(i, carry):
                at = pl.ds(i * group, group)
                red, blue, green, through = get(rel, at)
                first = plane_step(0, start + i * group, clear)
                put(rel, at, (
                    first[0] + first[3] * red, first[1] + first[3] * blue, first[2] + first[3] * green,
                    first[3] * through,
                ))
                return carry

            lax.fori_loop(0, groups, body, 0)

    def behind(rel, cond, low=0, high=groups):
        @pl.when(cond)
        def _():
            def body(i, carry):
                at, row = place(rel, i)
                put(rel, at, plane_step(last, row, get(rel, at)))
                return carry

            lax.fori_loop(low, high, body, 0)

    piece_copies = {}

    def forward(s, rel, i):
        j = rel >> (s + 1)
        slot = chips - (chips >> s) + j
        at, _ = place(rel, i)
        copy = remote(
            own.at[rel, :, at], pieces.at[slot, :, at], piece_send_sem.at[slot, i], piece_recv_sem.at[slot, i],
            opposite[s],
        )
        copy.start()
        piece_copies[s, j, i] = (copy, slot)

    for rel in order[:AHEAD]:
        near_part(rel, 0, groups - 1)
    def complete(step, rel, low, high):
        if low == high:
            return
        middle = min(high, groups - 1) if step < AHEAD else low
        if low < middle:
            far_part(rel, low, middle, False)
        if middle < high:
            far_part(rel, middle, high, True)
        if rel % 2:
            if rel == 1 and high == groups:
                in_front(rel, (odd == 1) & (core == 1))
            behind(rel, jnp.logical_not(has_behind), low, high)
            for i in range(low, high):
                forward(0, rel, i)

    swapped(0, order[0])
    for rel in odds:
        pass_on(rel)
    far_part(order[0], 0, groups - 1, False)
    edges(always)
    for kind in range(2):
        begin(has_next[kind] & has_beside & ((chip + core) % 2 == 1), halo(kind))
    behind(order[0], jnp.logical_not(has_behind), 0, groups - 1)
    for i in range(groups - 1):
        forward(0, order[0], i)
    complete(0, order[0], groups - 1, groups)
    for step, rel in enumerate(order[1:], 1):
        swapped(step, rel)
        complete(step, rel, 0, groups)

    def interfaces(rel):
        in_front(rel, has_front)
        if rel == 0:
            from_next(0, has_behind & ((odd == 1) | (core == 0)), rel)
            behind(rel, (odd == 1) | (core == 0))
        else:
            from_next(0, has_behind, rel)
            behind(rel, always)

    def received(s, j, i, state):
        rel = j << (s + 1)
        at, _ = place(rel, i)
        copy, slot = piece_copies[s, j, i]
        copy.wait_recv()
        return compose(chip // 2**s % 2 == 0, state, [pieces[slot, c, at] for c in range(4)])

    for s in range(stages):
        for j in reversed(range(1, chips >> (s + 1))):
            rel = j << (s + 1)
            if s == 0:
                interfaces(rel)
            for i in range(groups):
                at, _ = place(rel, i)
                put(rel, at, received(s, j, i, get(rel, at)))
                if j % 2:
                    forward(s + 1, rel, i)
    interfaces(0)
    drain()
    for i in range(groups):
        at, _ = place(0, i)
        state = get(0, at)
        for s in range(stages):
            state = received(s, 0, i, state)
        image = (0.5 * (state[0] + state[1]), state[2], 0.5 * (state[0] - state[1]), 1.0 - state[3])
        for c in range(4):
            result[at, c * SUB : (c + 1) * SUB, :] = image[c]
        for b in range(cols // LANE):
            out[at, :, b * LANE : (b + 1) * LANE] = result[at, pl.ds(b, 4, stride=SUB), :]

    for copy, _ in piece_copies.values():
        copy.wait_send()


def local(field):
    planes, rows, cols = field.shape
    depth_count = lax.axis_size("depth")
    chips = depth_count // 2
    share = rows // depth_count
    f32 = jnp.float32
    groups = min(share // g for g in range(1, 5) if share % g == 0)
    dims = (planes, rows, cols, depth_count, lax.axis_size("tile"), groups)
    dma = pltpu.SemaphoreType.DMA
    image = pl.pallas_call(
        functools.partial(kernel, dims),
        out_shape=jax.ShapeDtypeStruct((share, 4, cols), f32),
        in_specs=[pl.BlockSpec(memory_space=pltpu.HBM)],
        out_specs=pl.BlockSpec(memory_space=pltpu.VMEM),
        scratch_shapes=[
            pltpu.VMEM((2 * planes + 2, rows + 2, SUB, LANE), f32),
            pltpu.VMEM((chips, 4, share, SUB, LANE), f32),
            pltpu.VMEM((chips - 1, 4, share, SUB, LANE), f32),
            pltpu.VMEM((2, chips // 2, share + 2, SUB, LANE), f32),
            pltpu.VMEM((share, 4 * SUB, LANE), f32),
            dma((2, cols // LANE)),
            dma((chips,)),
            dma((chips,)),
            dma((2,)),
            dma((2,)),
            dma((2, chips)),
            dma((2, chips)),
            dma((2, chips // 2)),
            dma((2, chips // 2)),
            dma((2,)),
            dma((2,)),
            dma((chips - 1, groups)),
            dma((chips - 1, groups)),
        ],
        compiler_params=pltpu.CompilerParams(
            collective_id=0, has_side_effects=True, vmem_limit_bytes=55_000_000
        ),
    )(field)
    return jnp.transpose(image, (1, 0, 2))


def solution(mesh):
    return jax.shard_map(
        local,
        mesh=mesh,
        in_specs=(P("depth", "tile", None),),
        out_specs=P(None, ("tile", "depth"), None),
        check_vma=False,
    )
```
